256 devices in a mesh: tm: 8 (over z_lo, core), space: 32 (over z_hi, x, y).
Axes of the slice: x: 4, y: 4, z: 8 (z_hi: 2, z_lo: 4; z = z_hi * 4 + z_lo), core: 2. Of those that a mesh axis runs over, the one named last changes fastest.
Arguments:
- field_a: float32 [8, 8, 96, 18432], P('tm', None, 'space'), may hold values from -6 to 6
- field_b: float32 [8, 8, 96, 18432], P('tm', None, 'space'), may hold values from -6 to 6
- pairs: int32 [4, 16, 2], replicated, may hold values from 0 to 7
- signs: int32 [4, 16], replicated, may hold values from -1 to 1, as said below
Outputs:
- correlator: float32 [8, 4, 96, 18432], P('tm', None, 'space')
- first_diff: float32 [8, 4, 96, 18432], P('tm', None, 'space')
- second_diff: float32 [8, 4, 96, 18432], P('tm', None, 'space')
The draws below stay inside these ranges and needn't reach their ends.
Inputs may be any that keep to these rules, and one draw needn't show every extreme that they name: `signs`: each coefficient is -1 or 1.
All inputs are finite; a program needn't handle non-finite values.
Results may differ from the reference program's by a relative error of at most 0.0001.
Values sent between devices are 32-bit elements; how exact they have to be, the bound alone decides.
A program may use at most 192 MiB of HBM per device.

```python
import jax
import jax.numpy as jnp
from jax import lax

NX = 96
NY = 96
NZ = 96
NC = 8
NCH = 4
NPAIR = 16
TIMES = 8


def draw_signs(key, part):
    return (jax.random.randint(key, (NCH, NPAIR), 0, 2) * 2 - 1).astype(jnp.int32)


def place_ends(drawn, key, smallest, top_value):
    longest = drawn.shape.index(max(drawn.shape))
    spots = []
    for shift in (0, 1):
        where = [jax.random.randint(jax.random.fold_in(key, axis), (), 0, length) for axis, length in enumerate(drawn.shape)]
        where[longest] = (where[longest] + shift) % drawn.shape[longest]
        spots.append(tuple(where))
    return drawn.at[spots[0]].set(smallest).at[spots[1]].set(top_value)


def block_levels(rng, extent, pieces, low, largest):
    loudness = 1.0
    for axis_at, shards_of in pieces:
        heights = jax.random.uniform(jax.random.fold_in(jax.random.fold_in(rng, 6), axis_at), (shards_of,), jnp.float32, low / len(pieces), largest / len(pieces))
        loudness = loudness * jnp.repeat(jnp.exp(heights), extent[axis_at] // shards_of).reshape((-1,) + (1,) * (len(extent) - 1 - axis_at))
    return loudness


def bell_draw(rng, shape, scale, reach, split=(), kind=jnp.bfloat16):
    level = block_levels(rng, shape, split, -0.22, 0.18) if split else 1.0
    array = jax.random.normal(rng, shape, jnp.float32) * scale * level
    return jnp.minimum(jnp.maximum(array, -reach), reach).astype(kind)


def setup_inputs(seed: int = 0) -> dict:
    splits = jax.random.split(jax.random.key(seed), 5)
    field_a = bell_draw(splits[0], (TIMES, NC, NX, NY * 2 * NZ), 1.0, 6.0, ((0, 8), (2, 32)), jnp.float32)
    field_b = bell_draw(splits[1], (TIMES, NC, NX, NY * 2 * NZ), 1.0, 6.0, ((0, 8), (2, 32)), jnp.float32)
    pairs = place_ends(jax.random.randint(splits[2], (NCH, NPAIR, 2), 0, NC), jax.random.fold_in(splits[2], 1), 0, NC - 1).astype(jnp.int32)
    signs = draw_signs(jax.random.fold_in(splits[4], 71), 0)
    return dict(field_a=field_a, field_b=field_b, pairs=pairs, signs=signs)


def reference(field_a, field_b, pairs, signs):
    indices = jnp.arange(NC, dtype=jnp.int32)
    first = (pairs[:, :, 0][:, :, None] == indices[None, None, :]).astype(jnp.float32)
    second = (pairs[:, :, 1][:, :, None] == indices[None, None, :]).astype(jnp.float32)
    weights = jnp.einsum('cp,cpi,cpj->cij', signs.astype(jnp.float32), first, second)
    shaped_a = field_a.reshape(TIMES, NC, NX, NY, 2 * NZ)
    shaped_b = field_b.reshape(TIMES, NC, NX, NY, 2 * NZ)

    def one_slice(operands):
        slice_a, slice_b = operands
        comp_a = slice_a[..., :NZ] + 1j * slice_a[..., NZ:]
        comp_b = slice_b[..., :NZ] + 1j * slice_b[..., NZ:]
        hat_a = jnp.fft.fftn(comp_a, axes=(1, 2, 3), norm="ortho")
        hat_b = jnp.conj(jnp.fft.fftn(comp_b, axes=(1, 2, 3), norm="ortho"))
        outputs = []
        for channel in range(NCH):
            mixed_b = jnp.einsum('ij,jxyz->ixyz', weights[channel], hat_b)
            outputs.append(jnp.sum(hat_a * mixed_b, axis=0))
        mixed = jnp.stack(outputs, axis=0)
        result = jnp.fft.ifftn(mixed, axes=(1, 2, 3), norm="ortho")
        return jnp.concatenate([jnp.real(result), jnp.imag(result)], axis=-1).astype(jnp.float32)

    correlator = lax.map(one_slice, (shaped_a, shaped_b))
    correlator = correlator.reshape(TIMES, NCH, NX, NY * 2 * NZ)
    later = jnp.roll(correlator, -1, axis=0)
    earlier = jnp.roll(correlator, 1, axis=0)
    first_diff = later - correlator
    second_diff = later - 2.0 * correlator + earlier
    return correlator, first_diff, second_diff
```

```python
import functools
import math

import jax
import jax.numpy as jnp
import ml_dtypes
import numpy as np
from jax import lax
from jax.experimental import pallas as pl
from jax.experimental.pallas import tpu as pltpu
from jax.sharding import PartitionSpec as P

N = 96
PEERS = 32
MESH_ID = pl.DeviceIdType.MESH
F32 = jnp.float32
BF16 = jnp.bfloat16


def halves(table):
    high = table.astype(np.float32).astype(ml_dtypes.bfloat16)
    low = (table - high.astype(np.float64)).astype(np.float32).astype(ml_dtypes.bfloat16)
    return high, low


def trig(out_index, in_index):
    angle = (np.outer(out_index, in_index) % N) * (2.0 * math.pi / N)
    return np.cos(angle) / math.sqrt(N), np.sin(angle) / math.sqrt(N)


def left_table(out_index, in_index, in_parts, forward):
    cosines, sines = trig(out_index, in_index)
    turn = 1.0 if forward else -1.0
    real = np.where(in_parts[None, :] == 0, cosines, turn * sines)
    imag = np.where(in_parts[None, :] == 0, -turn * sines, cosines)
    return np.concatenate(halves(np.concatenate([real, imag], axis=0)), axis=0)


def plain_columns(index):
    return np.concatenate([index, index]), np.repeat([0, 1], N)


def tables():
    sites = np.arange(N)
    pairs_order = np.concatenate([2 * np.arange(48), 2 * np.arange(48) + 1])
    y_in = np.concatenate([2 * np.arange(48) + v for v in (0, 1) for _ in (0, 1)])
    y_parts = np.concatenate([np.full(48, part) for _ in (0, 1) for part in (0, 1)])
    dealt = np.concatenate([3 * np.arange(PEERS) + q for q in range(3)])
    forward_y = left_table(dealt, y_in, y_parts, True)
    forward_x = left_table(sites, *plain_columns(dealt), True)
    inverse_x = left_table(dealt, *plain_columns(sites), False)
    inverse_y = left_table(pairs_order, *plain_columns(dealt), False)
    cosines, sines = trig(sites, sites)
    forward_z = np.zeros((2, 256, 256))
    inverse_z = np.zeros((2, 256, 256))
    for v in (0, 1):
        rows = 64 * v
        forward_z[v, rows : rows + N, 0:N] = cosines
        forward_z[v, rows : rows + N, 128 : 128 + N] = -sines
        forward_z[v, rows + N : rows + 2 * N, 0:N] = sines
        forward_z[v, rows + N : rows + 2 * N, 128 : 128 + N] = cosines
        inverse_z[v, 0:N, rows : rows + N] = cosines
        inverse_z[v, 0:N, rows + N : rows + 2 * N] = sines
        inverse_z[v, 128 : 128 + N, rows : rows + N] = -sines
        inverse_z[v, 128 : 128 + N, rows + N : rows + 2 * N] = cosines
    fz = np.stack(halves(forward_z))
    iz = np.stack(halves(inverse_z))
    return forward_y, forward_x, inverse_x, inverse_y, fz, iz


def split(value):
    high = value.astype(BF16)
    return high, (value - high.astype(F32)).astype(BF16)


def mm(left, right):
    return jnp.dot(left, right, preferred_element_type=F32)


def apply_left(table, value):
    high, low = split(value)
    both = mm(table[...], high)
    return both[:192] + both[192:] + mm(table[0:192, :], low)


def apply_right(value, table, v):
    high, low = split(value)
    return mm(high, table[0, v]) + mm(low, table[0, v]) + mm(high, table[1, v])


def lanes(shape):
    return lax.broadcasted_iota(jnp.int32, shape, 1)


def depth_step(x_ref, x, fz, z_ref, slot):
    rows = jnp.concatenate([x_ref[x, :, 384 * u : 384 * u + 384] for u in range(48)], axis=0)
    for v in (0, 1):
        out = apply_right(rows[:, 128 * v : 128 * v + 256], fz, v)
        for part in (0, 1):
            z_ref[slot, x, 2 * v + part] = out[:, 128 * part : 128 * part + 128]


def rows_step(z_ref, fy, x, c, s_ref):
    sides = [
        jnp.concatenate([z_ref[f, x, i, pl.ds(c, 48, stride=8), :] for i in range(4)], axis=0)
        for f in (0, 1)
    ]
    out = apply_left(fy, jnp.concatenate(sides, axis=1))
    a_re, a_im = out[:96, :128], out[96:, :128]
    b_re, b_im = out[:96, 128:], out[96:, 128:]
    low = lanes((96, 128)) < 96
    packed = (
        jnp.where(low, a_re, pltpu.roll(b_im, 96, 1)),
        jnp.where(low, a_im, pltpu.roll(b_im, 64, 1)),
        jnp.where(low, b_re, pltpu.roll(b_im, 32, 1)),
    )
    for j in range(3):
        for q in range(3):
            s_ref[q, pl.ds((3 * j + x) * 8 + c, PEERS, stride=72), :] = packed[j][32 * q : 32 * q + 32]


def columns_step(r_ref, q, fx, c, h_ref):
    got = [
        jnp.concatenate(
            [r_ref[q, pl.ds((3 * j + x) * 8 + c, PEERS, stride=72), :] for x in range(3)], axis=0
        )
        for j in range(3)
    ]
    at = lanes((96, 128))
    b_im = jnp.where(
        at < 32, pltpu.roll(got[0], 32, 1), jnp.where(at < 64, pltpu.roll(got[1], 64, 1), pltpu.roll(got[2], 96, 1))
    )
    real = jnp.concatenate([got[0], got[2]], axis=1)
    imag = jnp.concatenate([got[1], b_im], axis=1)
    h_ref[c] = apply_left(fx, jnp.concatenate([real, imag], axis=0))


def contract_step(w_ref, h_ref, m_ref):
    @pl.loop(0, 12)
    def _(row):
        re = pl.ds(pl.multiple_of(row * 8, 8), 8)
        im = pl.ds(pl.multiple_of(row * 8 + 96, 8), 8)
        b_re = [h_ref[j, re, 128:] for j in range(8)]
        b_im = [h_ref[j, im, 128:] for j in range(8)]
        for ch in range(4):
            sum_re, sum_im = jnp.zeros((8, 128), F32), jnp.zeros((8, 128), F32)
            for i in range(8):
                mix_re = w_ref[ch * 64 + i * 8] * b_re[0]
                mix_im = w_ref[ch * 64 + i * 8] * b_im[0]
                for j in range(1, 8):
                    weight = w_ref[ch * 64 + i * 8 + j]
                    mix_re += weight * b_re[j]
                    mix_im += weight * b_im[j]
                a_re, a_im = h_ref[i, re, :128], h_ref[i, im, :128]
                sum_re += a_re * mix_re + a_im * mix_im
                sum_im += a_im * mix_re - a_re * mix_im
            m_ref[ch, re, :] = sum_re
            m_ref[ch, im, :] = sum_im


def columns_back_step(m_ref, ix, q, cs_ref):
    for pair in range(2):
        value = jnp.concatenate([m_ref[2 * pair], m_ref[2 * pair + 1]], axis=1)
        out = apply_left(ix, value)
        for k in range(2):
            ch = 2 * pair + k
            for part in range(2):
                for x in range(3):
                    at = 96 * part + 32 * x
                    cs_ref[q, pl.ds(8 * x + 4 * part + ch, PEERS, stride=24), :] = out[
                        at : at + 32, 128 * k : 128 * k + 128
                    ]


def rows_back_step(cr_ref, iy, x, pair, g_ref):
    sides = []
    for k in range(2):
        ch = 2 * pair + k
        sides.append(
            jnp.concatenate(
                [
                    cr_ref[q, pl.ds(8 * x + 4 * part + ch, PEERS, stride=24), :]
                    for part in range(2)
                    for q in range(3)
                ],
                axis=0,
            )
        )
    out = apply_left(iy, jnp.concatenate(sides, axis=1))
    for k in range(2):
        ch = 2 * pair + k
        for part in range(2):
            for v in range(2):
                at = 96 * part + 48 * v
                g_ref[x, 2 * v + part, pl.ds(ch, 48, stride=4), :] = out[at : at + 48, 128 * k : 128 * k + 128]


def depth_back_step(g_ref, iz, x, o_ref):
    outs = []
    for v in (0, 1):
        value = jnp.concatenate([g_ref[x, 2 * v], g_ref[x, 2 * v + 1]], axis=1)
        value = jnp.where(lax.rem(lanes((192, 256)), 128) < 96, value, 0.0)
        outs.append(apply_right(value, iz, v))
    o_ref[x, :, 0:128] = outs[0][:, :128]
    o_ref[x, :, 128:256] = outs[0][:, 128:] + outs[1][:, :128]
    o_ref[x, :, 256:384] = outs[1][:, 128:]


VMEM = pl.BlockSpec(memory_space=pltpu.VMEM)
SMEM = pl.BlockSpec(memory_space=pltpu.SMEM)
S_SHAPE = (3, PEERS * 72, 128)
C_SHAPE = (3, PEERS * 24, 128)
O_SHAPE = (3, 192, 384)


def params(**more):
    return pltpu.CompilerParams(vmem_limit_bytes=60_000_000, **more)


def forward_kernel(a_ref, b_ref, fz, fy, s_ref, z_ref):
    @pl.loop(0, 3)
    def _(x):
        depth_step(a_ref, x, fz, z_ref, 0)
        depth_step(b_ref, x, fz, z_ref, 1)

        @pl.loop(0, 8)
        def _(c):
            rows_step(z_ref, fy, x, c, s_ref)


def middle_kernel(w_ref, r_ref, fx, ix, cs_ref, h_ref, m_ref):
    @pl.loop(0, 3)
    def _(q):
        @pl.loop(0, 8)
        def _(c):
            columns_step(r_ref, q, fx, c, h_ref)

        contract_step(w_ref, h_ref, m_ref)
        columns_back_step(m_ref, ix, q, cs_ref)


def inverse_kernel(cr_ref, iy, iz, o_ref, g_ref):
    @pl.loop(0, 3)
    def _(x):
        for pair in range(2):
            rows_back_step(cr_ref, iy, x, pair, g_ref)
        depth_back_step(g_ref, iz, x, o_ref)


def exchange_kernel(rows, s_ref, r_ref, send_sem, recv_sem, own_sem):
    me, tm = lax.axis_index("space"), lax.axis_index("tm")
    barrier = pltpu.get_barrier_semaphore()
    for k in range(1, PEERS):
        pl.semaphore_signal(barrier, inc=1, device_id=(tm, lax.rem(me + k, PEERS)), device_id_type=MESH_ID)
    pl.semaphore_wait(barrier, PEERS - 1)
    mine = pl.ds(pl.multiple_of(me * rows, 8), rows)
    copies = []
    for k in range(1, PEERS):
        peer = lax.rem(me + k, PEERS)
        copy = pltpu.make_async_remote_copy(
            src_ref=s_ref.at[:, pl.ds(pl.multiple_of(peer * rows, 8), rows)],
            dst_ref=r_ref.at[:, mine],
            send_sem=send_sem.at[k],
            recv_sem=recv_sem.at[k],
            device_id=(tm, peer),
            device_id_type=MESH_ID,
        )
        copy.start()
        copies.append(copy)
    own = pltpu.make_async_copy(s_ref.at[:, mine], r_ref.at[:, mine], own_sem)
    own.start()
    own.wait()
    for copy in copies:
        copy.wait()


def times_kernel(o_ref, n_ref, send_sem, recv_sem):
    me, tm = lax.axis_index("space"), lax.axis_index("tm")
    barrier = pltpu.get_barrier_semaphore()
    near = (lax.rem(tm + 7, 8), lax.rem(tm + 1, 8))
    for k in range(2):
        pl.semaphore_signal(barrier, inc=1, device_id=(near[k], me), device_id_type=MESH_ID)
    pl.semaphore_wait(barrier, 2)
    copies = []
    for k in range(2):
        copy = pltpu.make_async_remote_copy(
            src_ref=o_ref,
            dst_ref=n_ref.at[k],
            send_sem=send_sem.at[k],
            recv_sem=recv_sem.at[k],
            device_id=(near[k], me),
            device_id_type=MESH_ID,
        )
        copy.start()
        copies.append(copy)
    for copy in copies:
        copy.wait()


def differences_kernel(o_ref, n_ref, c_ref, f_ref, d_ref):
    @pl.loop(0, 24)
    def _(pair):
        rows = pl.ds(pl.multiple_of(pair * 8, 8), 8)
        now, later, earlier = o_ref[0, rows, :], n_ref[0, 0, rows, :], n_ref[1, 0, rows, :]
        first = later - now
        second = later - 2.0 * now + earlier
        for half in range(2):
            out = pl.ds(pl.multiple_of(pair * 768 + half * 384, 128), 384)
            c_ref[0, :, out] = now[4 * half : 4 * half + 4]
            f_ref[0, :, out] = first[4 * half : 4 * half + 4]
            d_ref[0, :, out] = second[4 * half : 4 * half + 4]


def per_device(field_a, field_b, pairs, signs):
    components = field_a.shape[1]
    indices = jnp.arange(components, dtype=jnp.int32)
    first = (pairs[:, :, 0][:, :, None] == indices[None, None, :]).astype(F32)
    second = (pairs[:, :, 1][:, :, None] == indices[None, None, :]).astype(F32)
    weights = jnp.einsum("cp,cpi,cpj->cij", signs.astype(F32), first, second, precision=lax.Precision.HIGHEST)
    fy, fx, ix, iy, fz, iz = tables()
    a = jnp.transpose(field_a[0], (1, 0, 2))
    b = jnp.transpose(field_b[0], (1, 0, 2))
    sent = pl.pallas_call(
        forward_kernel,
        out_shape=jax.ShapeDtypeStruct(S_SHAPE, F32),
        in_specs=[VMEM] * 4,
        out_specs=VMEM,
        scratch_shapes=[pltpu.VMEM((2, 3, 4, 384, 128), F32)],
        compiler_params=params(),
        name="forward",
    )(a, b, fz, fy)

    def exchange(value, rows, number):
        return pl.pallas_call(
            functools.partial(exchange_kernel, rows),
            out_shape=jax.ShapeDtypeStruct(value.shape, F32),
            in_specs=[VMEM],
            out_specs=VMEM,
            scratch_shapes=[pltpu.SemaphoreType.DMA((PEERS,)), pltpu.SemaphoreType.DMA((PEERS,)), pltpu.SemaphoreType.DMA],
            compiler_params=params(collective_id=number, has_side_effects=True),
            name="exchange",
        )(value)

    received = exchange(sent, 72, 0)
    mixed = pl.pallas_call(
        middle_kernel,
        out_shape=jax.ShapeDtypeStruct(C_SHAPE, F32),
        in_specs=[SMEM] + [VMEM] * 3,
        out_specs=VMEM,
        scratch_shapes=[pltpu.VMEM((8, 192, 256), F32), pltpu.VMEM((4, 192, 128), F32)],
        compiler_params=params(),
        name="middle",
    )(weights.reshape(-1), received, fx, ix)
    returned = exchange(mixed, 24, 1)
    own = pl.pallas_call(
        inverse_kernel,
        out_shape=jax.ShapeDtypeStruct(O_SHAPE, F32),
        in_specs=[VMEM] * 3,
        out_specs=VMEM,
        scratch_shapes=[pltpu.VMEM((3, 4, 192, 128), F32)],
        compiler_params=params(),
        name="inverse",
    )(returned, iy, iz)
    near = pl.pallas_call(
        times_kernel,
        out_shape=jax.ShapeDtypeStruct((2,) + O_SHAPE, F32),
        in_specs=[VMEM],
        out_specs=VMEM,
        scratch_shapes=[pltpu.SemaphoreType.DMA((2,)), pltpu.SemaphoreType.DMA((2,))],
        compiler_params=params(collective_id=2, has_side_effects=True),
        name="times",
    )(own)
    block = pl.BlockSpec((1, 4, 18432), lambda x: (x, 0, 0))
    outs = pl.pallas_call(
        differences_kernel,
        grid=(3,),
        out_shape=[jax.ShapeDtypeStruct((3, 4, 18432), F32)] * 3,
        in_specs=[
            pl.BlockSpec((1, 192, 384), lambda x: (x, 0, 0)),
            pl.BlockSpec((2, 1, 192, 384), lambda x: (0, x, 0, 0)),
        ],
        out_specs=[block] * 3,
        compiler_params=params(),
        name="differences",
    )(own, near)
    return tuple(jnp.transpose(out, (1, 0, 2))[None] for out in outs)


def solution(mesh):
    spec = P("tm", None, "space", None)
    return jax.shard_map(
        per_device, mesh=mesh, in_specs=(spec, spec, P(), P()), out_specs=(spec,) * 3, check_vma=False
    )
```

```python
import math

import jax
import jax.numpy as jnp
import ml_dtypes
import numpy as np
from jax import lax
from jax.experimental import pallas as pl
from jax.experimental.pallas import tpu as pltpu
from jax.sharding import PartitionSpec as P

N = 96
PEERS = 32
MESH_ID = pl.DeviceIdType.MESH
F32 = jnp.float32
BF16 = jnp.bfloat16


def halves(table):
    high = table.astype(np.float32).astype(ml_dtypes.bfloat16)
    low = (table - high.astype(np.float64)).astype(np.float32).astype(ml_dtypes.bfloat16)
    return high, low


def trig(out_index, in_index):
    angle = (np.outer(out_index, in_index) % N) * (2.0 * math.pi / N)
    return np.cos(angle) / math.sqrt(N), np.sin(angle) / math.sqrt(N)


def left_table(out_index, in_index, in_parts, forward):
    cosines, sines = trig(out_index, in_index)
    turn = 1.0 if forward else -1.0
    real = np.where(in_parts[None, :] == 0, cosines, turn * sines)
    imag = np.where(in_parts[None, :] == 0, -turn * sines, cosines)
    return np.concatenate(halves(np.concatenate([real, imag], axis=0)), axis=0)


def plain_columns(index):
    return np.concatenate([index, index]), np.repeat([0, 1], N)


def tables():
    sites = np.arange(N)
    pairs_order = np.concatenate([2 * np.arange(48), 2 * np.arange(48) + 1])
    y_in = np.concatenate([2 * np.arange(48) + v for v in (0, 1) for _ in (0, 1)])
    y_parts = np.concatenate([np.full(48, part) for _ in (0, 1) for part in (0, 1)])
    dealt = np.concatenate([3 * np.arange(PEERS) + q for q in range(3)])
    forward_y = left_table(dealt, y_in, y_parts, True)
    forward_x = left_table(sites, *plain_columns(dealt), True)
    inverse_x = left_table(dealt, *plain_columns(sites), False)
    inverse_y = left_table(pairs_order, *plain_columns(dealt), False)
    cosines, sines = trig(sites, sites)
    forward_z = np.zeros((2, 256, 256))
    inverse_z = np.zeros((2, 256, 256))
    for v in (0, 1):
        rows = 64 * v
        forward_z[v, rows : rows + N, 0:N] = cosines
        forward_z[v, rows : rows + N, 128 : 128 + N] = -sines
        forward_z[v, rows + N : rows + 2 * N, 0:N] = sines
        forward_z[v, rows + N : rows + 2 * N, 128 : 128 + N] = cosines
        inverse_z[v, 0:N, rows : rows + N] = cosines
        inverse_z[v, 0:N, rows + N : rows + 2 * N] = sines
        inverse_z[v, 128 : 128 + N, rows : rows + N] = -sines
        inverse_z[v, 128 : 128 + N, rows + N : rows + 2 * N] = cosines
    fz = np.stack(halves(forward_z))
    iz = np.stack(halves(inverse_z))
    return forward_y, forward_x, inverse_x, inverse_y, fz, iz


def split(value):
    high = value.astype(BF16)
    return high, (value - high.astype(F32)).astype(BF16)


def mm(left, right):
    return jnp.dot(left, right, preferred_element_type=F32)


def apply_left(table, value):
    high, low = split(value)
    both = mm(table[...], high)
    return both[:192] + both[192:] + mm(table[0:192, :], low)


def apply_right(value, table, v):
    high, low = split(value)
    return mm(high, table[0, v]) + mm(low, table[0, v]) + mm(high, table[1, v])


def lanes(shape):
    return lax.broadcasted_iota(jnp.int32, shape, 1)


def depth_step(x_ref, x, fz, z_ref, slot):
    rows = jnp.concatenate([x_ref[x, :, 384 * u : 384 * u + 384] for u in range(48)], axis=0)
    for v in (0, 1):
        out = apply_right(rows[:, 128 * v : 128 * v + 256], fz, v)
        for part in (0, 1):
            z_ref[slot, x, 2 * v + part] = out[:, 128 * part : 128 * part + 128]


def rows_step(z_ref, fy, x, c, s_ref):
    sides = [
        jnp.concatenate([z_ref[f, x, i, pl.ds(c, 48, stride=8), :] for i in range(4)], axis=0)
        for f in (0, 1)
    ]
    out = apply_left(fy, jnp.concatenate(sides, axis=1))
    a_re, a_im = out[:96, :128], out[96:, :128]
    b_re, b_im = out[:96, 128:], out[96:, 128:]
    low = lanes((96, 128)) < 96
    packed = (
        jnp.where(low, a_re, pltpu.roll(b_im, 96, 1)),
        jnp.where(low, a_im, pltpu.roll(b_im, 64, 1)),
        jnp.where(low, b_re, pltpu.roll(b_im, 32, 1)),
    )
    for j in range(3):
        for q in range(3):
            s_ref[q, pl.ds((3 * x + j) * 8 + c, PEERS, stride=72), :] = packed[j][32 * q : 32 * q + 32]


def columns_step(r_ref, q, fx, c, h_ref):
    got = [
        jnp.concatenate(
            [r_ref[q, pl.ds((3 * x + j) * 8 + c, PEERS, stride=72), :] for x in range(3)], axis=0
        )
        for j in range(3)
    ]
    at = lanes((96, 128))
    b_im = jnp.where(
        at < 32, pltpu.roll(got[0], 32, 1), jnp.where(at < 64, pltpu.roll(got[1], 64, 1), pltpu.roll(got[2], 96, 1))
    )
    real = jnp.concatenate([got[0], got[2]], axis=1)
    imag = jnp.concatenate([got[1], b_im], axis=1)
    h_ref[c] = apply_left(fx, jnp.concatenate([real, imag], axis=0))


def contract_step(w_ref, h_ref, m_ref):
    @pl.loop(0, 12)
    def _(row):
        re = pl.ds(pl.multiple_of(row * 8, 8), 8)
        im = pl.ds(pl.multiple_of(row * 8 + 96, 8), 8)
        b_re = [h_ref[j, re, 128:] for j in range(8)]
        b_im = [h_ref[j, im, 128:] for j in range(8)]
        for ch in range(4):
            sum_re, sum_im = jnp.zeros((8, 128), F32), jnp.zeros((8, 128), F32)
            for i in range(8):
                mix_re = w_ref[ch * 64 + i * 8] * b_re[0]
                mix_im = w_ref[ch * 64 + i * 8] * b_im[0]
                for j in range(1, 8):
                    weight = w_ref[ch * 64 + i * 8 + j]
                    mix_re += weight * b_re[j]
                    mix_im += weight * b_im[j]
                a_re, a_im = h_ref[i, re, :128], h_ref[i, im, :128]
                sum_re += a_re * mix_re + a_im * mix_im
                sum_im += a_im * mix_re - a_re * mix_im
            m_ref[ch, re, :] = sum_re
            m_ref[ch, im, :] = sum_im


def columns_back_step(m_ref, ix, q, cs_ref):
    for pair in range(2):
        value = jnp.concatenate([m_ref[2 * pair], m_ref[2 * pair + 1]], axis=1)
        out = apply_left(ix, value)
        for k in range(2):
            ch = 2 * pair + k
            for part in range(2):
                for x in range(3):
                    at = 96 * part + 32 * x
                    cs_ref[q, pl.ds(8 * x + 4 * part + ch, PEERS, stride=24), :] = out[
                        at : at + 32, 128 * k : 128 * k + 128
                    ]


def rows_back_step(cr_ref, iy, x, pair, g_ref):
    sides = []
    for k in range(2):
        ch = 2 * pair + k
        sides.append(
            jnp.concatenate(
                [
                    cr_ref[q, pl.ds(8 * x + 4 * part + ch, PEERS, stride=24), :]
                    for part in range(2)
                    for q in range(3)
                ],
                axis=0,
            )
        )
    out = apply_left(iy, jnp.concatenate(sides, axis=1))
    for k in range(2):
        ch = 2 * pair + k
        for part in range(2):
            for v in range(2):
                at = 96 * part + 48 * v
                g_ref[x, 2 * v + part, pl.ds(ch, 48, stride=4), :] = out[at : at + 48, 128 * k : 128 * k + 128]


def depth_back_step(g_ref, iz, x, o_ref):
    outs = []
    for v in (0, 1):
        value = jnp.concatenate([g_ref[x, 2 * v], g_ref[x, 2 * v + 1]], axis=1)
        value = jnp.where(lax.rem(lanes((192, 256)), 128) < 96, value, 0.0)
        outs.append(apply_right(value, iz, v))
    o_ref[x, :, 0:128] = outs[0][:, :128]
    o_ref[x, :, 128:256] = outs[0][:, 128:] + outs[1][:, :128]
    o_ref[x, :, 256:384] = outs[1][:, 128:]


VMEM = pl.BlockSpec(memory_space=pltpu.VMEM)
SMEM = pl.BlockSpec(memory_space=pltpu.SMEM)
ANY = pl.BlockSpec(memory_space=pl.ANY)


def difference_step(o_ref, n_ref, out_ref, x):
    for pair in range(24):
        rows = pl.ds(pair * 8, 8)
        now, later, earlier = o_ref[x, rows, :], n_ref[0, x, rows, :], n_ref[1, x, rows, :]
        first = later - now
        second = later - 2.0 * now + earlier
        for half in range(2):
            at = pl.ds(pair * 768 + half * 384, 384)
            out_ref[0, x, :, at] = now[4 * half : 4 * half + 4]
            out_ref[1, x, :, at] = first[4 * half : 4 * half + 4]
            out_ref[2, x, :, at] = second[4 * half : 4 * half + 4]


def whole_kernel(
    a_hbm, b_hbm, w_ref, fz, fy, fx, ix, iy, iz,
    c_hbm, f_hbm, d_hbm,
    ab_ref, z_ref, s_ref, r_ref, h_ref, m_ref, cs_ref, cr_ref, g_ref, o_ref, n_ref, out_ref,
    in_sem, out_sem, own_sem, fs_sem, fr_sem, cs_sem, cr_sem, ts_sem, tr_sem,
):
    me, tm = lax.axis_index("space"), lax.axis_index("tm")
    near = (lax.rem(tm + 7, 8), lax.rem(tm + 1, 8))

    def load(f, x):
        return pltpu.make_async_copy((a_hbm, b_hbm)[f].at[x], ab_ref.at[f, x], in_sem.at[f, x])

    for x in range(3):
        for f in range(2):
            load(f, x).start()
    barrier = pltpu.get_barrier_semaphore()

    @pl.loop(1, PEERS)
    def _(k):
        pl.semaphore_signal(barrier, inc=1, device_id=(tm, lax.rem(me + k, PEERS)), device_id_type=MESH_ID)

    for k in range(2):
        pl.semaphore_signal(barrier, inc=1, device_id=(near[k], me), device_id_type=MESH_ID)

    def forward_copy(k, q, first, rows, part):
        peer = lax.rem(me + k, PEERS)
        return pltpu.make_async_remote_copy(
            src_ref=s_ref.at[q, pl.ds(pl.multiple_of(peer * 72 + first, 8), rows)],
            dst_ref=r_ref.at[q, pl.ds(pl.multiple_of(me * 72 + first, 8), rows)],
            send_sem=fs_sem.at[part, k],
            recv_sem=fr_sem.at[part, k],
            device_id=(tm, peer),
            device_id_type=MESH_ID,
        )

    def own_forward(q):
        at = pl.ds(pl.multiple_of(me * 72, 8), 72)
        return pltpu.make_async_copy(s_ref.at[q, at], r_ref.at[q, at], own_sem.at[q])

    def back_copy(k, q):
        peer = lax.rem(me + k, PEERS)
        return pltpu.make_async_remote_copy(
            src_ref=cs_ref.at[q, pl.ds(pl.multiple_of(peer * 24, 8), 24)],
            dst_ref=cr_ref.at[q, pl.ds(pl.multiple_of(me * 24, 8), 24)],
            send_sem=cs_sem.at[q, k],
            recv_sem=cr_sem.at[q, k],
            device_id=(tm, peer),
            device_id_type=MESH_ID,
        )

    def own_back(q):
        at = pl.ds(pl.multiple_of(me * 24, 8), 24)
        return pltpu.make_async_copy(cs_ref.at[q, at], cr_ref.at[q, at], own_sem.at[3 + q])

    def time_copy(k, x):
        return pltpu.make_async_remote_copy(
            src_ref=o_ref.at[x],
            dst_ref=n_ref.at[k, x],
            send_sem=ts_sem.at[k, x],
            recv_sem=tr_sem.at[k, x],
            device_id=(near[k], me),
            device_id_type=MESH_ID,
        )

    def each_peer(act):
        @pl.loop(1, PEERS)
        def _(k):
            act(k)

    @pl.loop(0, 3)
    def _(x):
        for f in range(2):
            load(f, x).wait()
            depth_step(ab_ref.at[f], x, fz, z_ref, f)

        @pl.loop(0, 8)
        def _(c):
            rows_step(z_ref, fy, x, c, s_ref)

        @pl.when(x == 0)
        def _():
            pl.semaphore_wait(barrier, PEERS + 1)

        each_peer(lambda k: forward_copy(k, 0, 24 * x, 24, x).start())

    for q in (1, 2):
        each_peer(lambda k: forward_copy(k, q, 0, 72, 2 + q).start())
    for q in range(3):
        own_forward(q).start()

    for q in range(3):
        own_forward(q).wait()
        if q == 0:
            for x in range(3):
                each_peer(lambda k: forward_copy(k, 0, 24 * x, 24, x).wait_recv())
        else:
            each_peer(lambda k: forward_copy(k, q, 0, 72, 2 + q).wait_recv())

        @pl.loop(0, 8)
        def _(c):
            columns_step(r_ref, q, fx, c, h_ref)

        contract_step(w_ref, h_ref, m_ref)
        columns_back_step(m_ref, ix, q, cs_ref)
        each_peer(lambda k: back_copy(k, q).start())
        own_back(q).start()

    for q in range(3):
        own_back(q).wait()
        each_peer(lambda k: back_copy(k, q).wait_recv())

    @pl.loop(0, 3)
    def _(x):
        for pair in range(2):
            rows_back_step(cr_ref, iy, x, pair, g_ref)
        depth_back_step(g_ref, iz, x, o_ref)
        for k in range(2):
            time_copy(k, x).start()

    def store(i, x):
        return pltpu.make_async_copy(out_ref.at[i, x], (c_hbm, f_hbm, d_hbm)[i].at[x], out_sem.at[i, x])

    @pl.loop(0, 3)
    def _(x):
        for k in range(2):
            time_copy(k, x).wait_recv()
        difference_step(o_ref, n_ref, out_ref, x)
        for i in range(3):
            store(i, x).start()

    for x in range(3):
        each_peer(lambda k: forward_copy(k, 0, 24 * x, 24, x).wait_send())
    for q in (1, 2):
        each_peer(lambda k: forward_copy(k, q, 0, 72, 2 + q).wait_send())
    for q in range(3):
        each_peer(lambda k: back_copy(k, q).wait_send())
    for x in range(3):
        for k in range(2):
            time_copy(k, x).wait_send()
        for i in range(3):
            store(i, x).wait()


def per_device(field_a, field_b, pairs, signs):
    components = field_a.shape[1]
    indices = jnp.arange(components, dtype=jnp.int32)
    first = (pairs[:, :, 0][:, :, None] == indices[None, None, :]).astype(F32)
    second = (pairs[:, :, 1][:, :, None] == indices[None, None, :]).astype(F32)
    weights = jnp.einsum("cp,cpi,cpj->cij", signs.astype(F32), first, second, precision=lax.Precision.HIGHEST)
    fy, fx, ix, iy, fz, iz = tables()
    a = jnp.transpose(field_a[0], (1, 0, 2))
    b = jnp.transpose(field_b[0], (1, 0, 2))
    dma = pltpu.SemaphoreType.DMA
    outs = pl.pallas_call(
        whole_kernel,
        out_shape=[jax.ShapeDtypeStruct((3, 4, 18432), F32)] * 3,
        in_specs=[ANY, ANY, SMEM] + [VMEM] * 6,
        out_specs=[ANY] * 3,
        scratch_shapes=[
            pltpu.VMEM((2, 3, 8, 18432), F32),
            pltpu.VMEM((2, 3, 4, 384, 128), F32),
            pltpu.VMEM((3, PEERS * 72, 128), F32),
            pltpu.VMEM((3, PEERS * 72, 128), F32),
            pltpu.VMEM((8, 192, 256), F32),
            pltpu.VMEM((4, 192, 128), F32),
            pltpu.VMEM((3, PEERS * 24, 128), F32),
            pltpu.VMEM((3, PEERS * 24, 128), F32),
            pltpu.VMEM((3, 4, 192, 128), F32),
            pltpu.VMEM((3, 192, 384), F32),
            pltpu.VMEM((2, 3, 192, 384), F32),
            pltpu.VMEM((3, 3, 4, 18432), F32),
            dma((2, 3)),
            dma((3, 3)),
            dma((6,)),
            dma((5, PEERS)),
            dma((5, PEERS)),
            dma((3, PEERS)),
            dma((3, PEERS)),
            dma((2, 3)),
            dma((2, 3)),
        ],
        compiler_params=pltpu.CompilerParams(vmem_limit_bytes=60_000_000, collective_id=0, has_side_effects=True),
        name="whole",
    )(a, b, weights.reshape(-1), fz, fy, fx, ix, iy, iz)
    return tuple(jnp.transpose(out, (1, 0, 2))[None] for out in outs)


def solution(mesh):
    spec = P("tm", None, "space", None)
    return jax.shard_map(
        per_device, mesh=mesh, in_specs=(spec, spec, P(), P()), out_specs=(spec,) * 3, check_vma=False
    )
```

```python
import math

import jax
import jax.numpy as jnp
import ml_dtypes
import numpy as np
from jax import lax
from jax.experimental import pallas as pl
from jax.experimental.pallas import tpu as pltpu
from jax.sharding import PartitionSpec as P

N = 96
PEERS = 32
CELLS = 16
MESH_ID = pl.DeviceIdType.MESH
F32 = jnp.float32
BF16 = jnp.bfloat16


def halves(table):
    high = table.astype(np.float32).astype(ml_dtypes.bfloat16)
    low = (table - high.astype(np.float64)).astype(np.float32).astype(ml_dtypes.bfloat16)
    return high, low


def trig(out_index, in_index):
    angle = (np.outer(out_index, in_index) % N) * (2.0 * math.pi / N)
    return np.cos(angle) / math.sqrt(N), np.sin(angle) / math.sqrt(N)


def left_table(out_index, in_index, in_parts, forward):
    cosines, sines = trig(out_index, in_index)
    turn = 1.0 if forward else -1.0
    real = np.where(in_parts[None, :] == 0, cosines, turn * sines)
    imag = np.where(in_parts[None, :] == 0, -turn * sines, cosines)
    return np.concatenate(halves(np.concatenate([real, imag], axis=0)), axis=0)


def plain_columns(index):
    return np.concatenate([index, index]), np.repeat([0, 1], N)


def tables():
    sites = np.arange(N)
    pairs_order = np.concatenate([2 * np.arange(48), 2 * np.arange(48) + 1])
    y_in = np.concatenate([2 * np.arange(48) + v for v in (0, 1) for _ in (0, 1)])
    y_parts = np.concatenate([np.full(48, part) for _ in (0, 1) for part in (0, 1)])
    dealt = np.concatenate([3 * np.arange(PEERS) + q for q in range(3)])
    forward_y = left_table(dealt, y_in, y_parts, True)
    forward_x = left_table(sites, *plain_columns(dealt), True)
    inverse_x = left_table(dealt, *plain_columns(sites), False)
    inverse_y = left_table(pairs_order, *plain_columns(dealt), False)
    cosines, sines = trig(sites, sites)
    forward_z = np.zeros((2, 256, 256))
    inverse_z = np.zeros((2, 256, 256))
    for v in (0, 1):
        rows = 64 * v
        forward_z[v, rows : rows + N, 0:N] = cosines
        forward_z[v, rows : rows + N, 128 : 128 + N] = -sines
        forward_z[v, rows + N : rows + 2 * N, 0:N] = sines
        forward_z[v, rows + N : rows + 2 * N, 128 : 128 + N] = cosines
        inverse_z[v, 0:N, rows : rows + N] = cosines
        inverse_z[v, 0:N, rows + N : rows + 2 * N] = sines
        inverse_z[v, 128 : 128 + N, rows : rows + N] = -sines
        inverse_z[v, 128 : 128 + N, rows + N : rows + 2 * N] = cosines
    fz = np.stack(halves(forward_z))
    iz = np.stack(halves(inverse_z))
    return forward_y, forward_x, inverse_x, inverse_y, fz, iz


def split(value):
    high = value.astype(BF16)
    return high, (value - high.astype(F32)).astype(BF16)


def mm(left, right):
    return jnp.dot(left, right, preferred_element_type=F32)


def apply_left(table, value):
    high, low = split(value)
    both = mm(table[...], high)
    return both[:192] + both[192:] + mm(table[0:192, :], low)


def apply_right(value, table, v):
    high, low = split(value)
    return mm(high, table[0, v]) + mm(low, table[0, v]) + mm(high, table[1, v])


def lanes(shape):
    return lax.broadcasted_iota(jnp.int32, shape, 1)


def depth_step(x_ref, x, fz, z_ref, slot):
    rows = jnp.concatenate([x_ref[x, :, 384 * u : 384 * u + 384] for u in range(48)], axis=0)
    for v in (0, 1):
        out = apply_right(rows[:, 128 * v : 128 * v + 256], fz, v)
        for part in (0, 1):
            z_ref[slot, x, 2 * v + part] = out[:, 128 * part : 128 * part + 128]


def rows_step(z_ref, fy, x, c, s_ref):
    sides = [
        jnp.concatenate([z_ref[f, x, i, pl.ds(c, 48, stride=8), :] for i in range(4)], axis=0)
        for f in (0, 1)
    ]
    out = apply_left(fy, jnp.concatenate(sides, axis=1))
    a_re, a_im = out[:96, :128], out[96:, :128]
    b_re, b_im = out[:96, 128:], out[96:, 128:]
    low = lanes((96, 128)) < 96
    packed = (
        jnp.where(low, a_re, pltpu.roll(b_im, 96, 1)),
        jnp.where(low, a_im, pltpu.roll(b_im, 64, 1)),
        jnp.where(low, b_re, pltpu.roll(b_im, 32, 1)),
    )
    for j in range(3):
        for q in range(3):
            s_ref[q, x, pl.ds(8 * j + c, PEERS, stride=24), :] = packed[j][32 * q : 32 * q + 32]


def columns_step(r_ref, q, fx, c, h_ref):
    got = [
        jnp.concatenate(
            [r_ref[q, x, pl.ds(8 * j + c, PEERS, stride=24), :] for x in range(3)], axis=0
        )
        for j in range(3)
    ]
    at = lanes((96, 128))
    b_im = jnp.where(
        at < 32, pltpu.roll(got[0], 32, 1), jnp.where(at < 64, pltpu.roll(got[1], 64, 1), pltpu.roll(got[2], 96, 1))
    )
    real = jnp.concatenate([got[0], got[2]], axis=1)
    imag = jnp.concatenate([got[1], b_im], axis=1)
    h_ref[c] = apply_left(fx, jnp.concatenate([real, imag], axis=0))


def weights_step(pairs_ref, signs_ref, w_ref):
    row = lax.broadcasted_iota(jnp.int32, (8, 128), 0)
    lane = lax.broadcasted_iota(jnp.int32, (8, 128), 1)

    @pl.loop(0, 4)
    def _(ch):
        total = jnp.zeros((8, 128), F32)
        for p in range(16):
            here = (row == pairs_ref[ch, 0, p]) & (lane == pairs_ref[ch, 1, p])
            total += jnp.where(here, signs_ref[ch, p].astype(F32), 0.0)
        for i in range(8):
            for j in range(8):
                w_ref[64 * ch + 8 * i + j] = jnp.broadcast_to(total[i : i + 1, j : j + 1], (8, 128))


def contract_step(w_ref, h_ref, m_ref):
    @pl.loop(0, 12)
    def _(row):
        re = pl.ds(pl.multiple_of(row * 8, 8), 8)
        im = pl.ds(pl.multiple_of(row * 8 + 96, 8), 8)
        b_re = [h_ref[j, re, 128:] for j in range(8)]
        b_im = [h_ref[j, im, 128:] for j in range(8)]

        @pl.loop(0, 4)
        def _(ch):
            sum_re, sum_im = jnp.zeros((8, 128), F32), jnp.zeros((8, 128), F32)
            for i in range(8):
                weight = w_ref[ch * 64 + i * 8]
                mix_re = weight * b_re[0]
                mix_im = weight * b_im[0]
                for j in range(1, 8):
                    weight = w_ref[ch * 64 + i * 8 + j]
                    mix_re += weight * b_re[j]
                    mix_im += weight * b_im[j]
                a_re, a_im = h_ref[i, re, :128], h_ref[i, im, :128]
                sum_re += a_re * mix_re + a_im * mix_im
                sum_im += a_im * mix_re - a_re * mix_im
            m_ref[ch, re, :] = sum_re
            m_ref[ch, im, :] = sum_im


def columns_back_step(m_ref, ix, q, cs0_ref, cs_ref, k_ref):
    at = lanes((32, 128))
    for pair in range(2):
        value = jnp.concatenate([m_ref[2 * pair], m_ref[2 * pair + 1]], axis=1)
        out = apply_left(ix, value)

        def block(k, part, x):
            first = 96 * part + 32 * x
            return out[first : first + 32, 128 * k : 128 * k + 128]

        @pl.when(q == 0)
        def _():
            for k in range(2):
                for part in range(2):
                    row = 4 * part + 2 * pair + k
                    got = [block(k, part, x) for x in range(3)]
                    for x in range(3):
                        k_ref[0, 8 * x + row] = pltpu.roll(got[x], 96, 1)
                        k_ref[1, 8 * x + row] = pltpu.roll(got[x], 64, 1)
                    cs0_ref[pl.ds(row, PEERS, stride=8), :] = jnp.where(
                        at < 32, pltpu.roll(got[0], 64, 1), jnp.where(at < 64, pltpu.roll(got[1], 96, 1), got[2])
                    )

        @pl.when(q > 0)
        def _():
            for k in range(2):
                for part in range(2):
                    for x in range(3):
                        row = 8 * x + 4 * part + 2 * pair + k
                        cs_ref[q - 1, pl.ds(row, PEERS, stride=24), :] = jnp.where(
                            at < 96, block(k, part, x), k_ref[q - 1, row]
                        )


def rows_back_step(cr0_ref, cr_ref, iy, x, pair, g_ref):
    at = lanes((32, 128))
    sides = []
    for k in range(2):
        ch = 2 * pair + k
        parts = []
        for part in range(2):
            own = cr0_ref[pl.ds(4 * part + ch, PEERS, stride=8), :]
            second, third = (cr_ref[i, pl.ds(8 * x + 4 * part + ch, PEERS, stride=24), :] for i in range(2))
            first = jnp.where(
                at < 32,
                pltpu.roll(second, 32, 1),
                jnp.where(at < 64, pltpu.roll(third, 64, 1), pltpu.roll(own, (64 - 32 * x) % 128, 1)),
            )
            parts += [first, second, third]
        sides.append(jnp.concatenate(parts, axis=0))
    out = apply_left(iy, jnp.concatenate(sides, axis=1))
    for k in range(2):
        ch = 2 * pair + k
        for part in range(2):
            for v in range(2):
                first = 96 * part + 48 * v
                g_ref[x, 2 * v + part, pl.ds(ch, 48, stride=4), :] = out[
                    first : first + 48, 128 * k : 128 * k + 128
                ]


def depth_back_step(g_ref, iz, x, o_ref):
    outs = []
    for v in (0, 1):
        value = jnp.concatenate([g_ref[x, 2 * v], g_ref[x, 2 * v + 1]], axis=1)
        value = jnp.where(lax.rem(lanes((192, 256)), 128) < 96, value, 0.0)
        outs.append(apply_right(value, iz, v))
    o_ref[x, :, 0:128] = outs[0][:, :128]
    o_ref[x, :, 128:256] = outs[0][:, 128:] + outs[1][:, :128]
    o_ref[x, :, 256:384] = outs[1][:, 128:]


VMEM = pl.BlockSpec(memory_space=pltpu.VMEM)
SMEM = pl.BlockSpec(memory_space=pltpu.SMEM)
ANY = pl.BlockSpec(memory_space=pl.ANY)


def difference_step(o_ref, n_ref, out_ref, x):
    for pair in range(24):
        rows = pl.ds(pair * 8, 8)
        now, later, earlier = o_ref[x, rows, :], n_ref[0, x, rows, :], n_ref[1, x, rows, :]
        first = later - now
        second = later - 2.0 * now + earlier
        for half in range(2):
            at = pl.ds(pair * 768 + half * 384, 384)
            out_ref[0, x, :, at] = now[4 * half : 4 * half + 4]
            out_ref[1, x, :, at] = first[4 * half : 4 * half + 4]
            out_ref[2, x, :, at] = second[4 * half : 4 * half + 4]


def whole_kernel(
    a_hbm, b_hbm, pairs_ref, signs_ref, fz, fy, fx, ix, iy, iz,
    c_hbm, f_hbm, d_hbm,
    ab_ref, z_ref, s_ref, t_ref, r_ref, h_ref, m_ref, w_ref, k_ref, cs0_ref, cs_ref, ct0_ref, ct_ref, cr0_ref, cr_ref, g_ref, o_ref, n_ref, out_ref,
    in_sem, out_sem, own_sem, zs_sem, zr_sem, fs_sem, fr_sem, bs_sem, br_sem, cs_sem, cr_sem, ts_sem, tr_sem,
):
    me, tm = lax.axis_index("space"), lax.axis_index("tm")
    near = (lax.rem(tm + 7, 8), lax.rem(tm + 1, 8))
    half, cell = me // CELLS, lax.rem(me, CELLS)
    partner = lax.rem(me + CELLS, PEERS)
    far = (1 - half) * CELLS

    def cell_of(k):
        along_x = lax.rem(cell // 4 + k // 4, 4)
        along_y = lax.rem(lax.rem(cell, 4) + lax.rem(k, 4), 4)
        return 4 * along_x + along_y

    def rows(first, count=1):
        return pl.ds(pl.multiple_of(first * 24, 8), count * 24)

    def remote(src, dst, send, recv, space, time=None):
        return pltpu.make_async_remote_copy(
            src_ref=src,
            dst_ref=dst,
            send_sem=send,
            recv_sem=recv,
            device_id=(tm if time is None else time, space),
            device_id_type=MESH_ID,
        )

    def each_cell(act):
        @pl.loop(1, CELLS)
        def _(k):
            act(cell_of(k))

    def load(f, x):
        return pltpu.make_async_copy((a_hbm, b_hbm)[f].at[x], ab_ref.at[f, x], in_sem.at[f, x])

    for x in range(3):
        for f in range(2):
            load(f, x).start()
    barrier = pltpu.get_barrier_semaphore()
    pl.semaphore_signal(barrier, inc=1, device_id=(tm, partner), device_id_type=MESH_ID)
    each_cell(
        lambda to: pl.semaphore_signal(
            barrier, inc=1, device_id=(tm, half * CELLS + to), device_id_type=MESH_ID
        )
    )
    for k in range(2):
        pl.semaphore_signal(barrier, inc=1, device_id=(near[k], me), device_id_type=MESH_ID)

    def cross(q, x):
        return remote(s_ref.at[q, x, rows(far, CELLS)], t_ref.at[q, x], zs_sem.at[q, x], zr_sem.at[q, x], partner)

    def spread(q, x, to):
        at = half * CELLS + to
        return remote(s_ref.at[q, x, rows(at)], r_ref.at[q, x, rows(me)], fs_sem.at[0], fr_sem.at[0, q], at)

    def relay(q, x, to):
        at = half * CELLS + to
        return remote(t_ref.at[q, x, rows(to)], r_ref.at[q, x, rows(partner)], fs_sem.at[1], fr_sem.at[1, q], at)

    def keep(q, x):
        return pltpu.make_async_copy(s_ref.at[q, x, rows(me)], r_ref.at[q, x, rows(me)], own_sem.at[0, q, x])

    def keep_relay(q, x):
        return pltpu.make_async_copy(t_ref.at[q, x, rows(cell)], r_ref.at[q, x, rows(partner)], own_sem.at[1, q, x])

    def group(refs, g, first, count=1):
        size = 24 if g else 8
        at = pl.ds(pl.multiple_of(first * size, 8), count * size)
        return refs[1].at[g - 1, at] if g else refs[0].at[at]

    made, passed, final = (cs0_ref, cs_ref), (ct0_ref, ct_ref), (cr0_ref, cr_ref)

    def cross_back(g):
        return remote(group(made, g, far, CELLS), group(passed, g, 0, CELLS), bs_sem.at[g], br_sem.at[g], partner)

    def spread_back(g, to):
        at = half * CELLS + to
        return remote(group(made, g, at), group(final, g, me), cs_sem.at[0, g], cr_sem.at[0, g], at)

    def relay_back(g, to):
        at = half * CELLS + to
        return remote(group(passed, g, to), group(final, g, partner), cs_sem.at[1, g], cr_sem.at[1, g], at)

    def all_back(i, g):
        some = group(final, g, 0, CELLS - 1)
        return remote(some, some, cs_sem.at[i, g], cr_sem.at[i, g], partner)

    def keep_back(g):
        return pltpu.make_async_copy(group(made, g, me), group(final, g, me), own_sem.at[2, g, 0])

    def keep_relay_back(g):
        return pltpu.make_async_copy(group(passed, g, cell), group(final, g, partner), own_sem.at[2, g, 1])

    def send_back(g):
        cross_back(g).start()
        each_cell(lambda to: spread_back(g, to).start())
        keep_back(g).start()

    def time_copy(k, x):
        return remote(o_ref.at[x], n_ref.at[k, x], ts_sem.at[k, x], tr_sem.at[k, x], me, near[k])

    def send(q, x):
        cross(q, x).start()
        each_cell(lambda to: spread(q, x, to).start())
        keep(q, x).start()

    @pl.loop(0, 3)
    def _(x):
        for f in range(2):
            load(f, x).wait()
            depth_step(ab_ref.at[f], x, fz, z_ref, f)

        @pl.loop(0, 8)
        def _(c):
            rows_step(z_ref, fy, x, c, s_ref)

        @pl.when(x == 0)
        def _():
            pl.semaphore_wait(barrier, CELLS + 2)

        send(0, x)

    @pl.loop(0, 6)
    def _(i):
        send(1 + i // 3, lax.rem(i, 3))

    every = pl.ds(0, 24 * (CELLS - 1))
    weights_step(pairs_ref, signs_ref, w_ref)

    @pl.loop(0, 3)
    def _(q):
        @pl.loop(0, 3)
        def _(x):
            cross(q, x).wait_recv()
            each_cell(lambda to: relay(q, x, to).start())
            keep_relay(q, x).start()
            keep(q, x).wait()

        for i in range(2):
            remote(r_ref.at[q, :, every], r_ref.at[q, :, every], fs_sem.at[i], fr_sem.at[i, q], partner).wait_recv()

        @pl.loop(0, 3)
        def _(x):
            keep_relay(q, x).wait()

        @pl.loop(0, 8)
        def _(c):
            columns_step(r_ref, q, fx, c, h_ref)

        contract_step(w_ref, h_ref, m_ref)
        columns_back_step(m_ref, ix, q, cs0_ref, cs_ref, k_ref)
        for g in range(3):

            @pl.when(q == g)
            def _():
                send_back(g)

    for g in range(3):
        cross_back(g).wait_recv()
        each_cell(lambda to: relay_back(g, to).start())
        keep_relay_back(g).start()
        keep_back(g).wait()
    for g in range(3):
        for i in range(2):
            all_back(i, g).wait_recv()
        keep_relay_back(g).wait()

    for x in range(3):
        for pair in range(2):
            rows_back_step(cr0_ref, cr_ref, iy, x, pair, g_ref)
        depth_back_step(g_ref, iz, x, o_ref)
        for k in range(2):
            time_copy(k, x).start()

    def store(i, x):
        return pltpu.make_async_copy(out_ref.at[i, x], (c_hbm, f_hbm, d_hbm)[i].at[x], out_sem.at[i, x])

    @pl.loop(0, 3)
    def _(x):
        for k in range(2):
            time_copy(k, x).wait_recv()
        difference_step(o_ref, n_ref, out_ref, x)
        for i in range(3):
            store(i, x).start()

    for i in range(2):
        remote(s_ref.at[:, :, every], s_ref.at[:, :, every], fs_sem.at[i], fr_sem.at[i, 0], partner).wait_send()
        for g in range(3):
            all_back(i, g).wait_send()
    for g in range(3):
        cross_back(g).wait_send()

    @pl.loop(0, 3)
    def _(q):
        for x in range(3):
            cross(q, x).wait_send()
        for k in range(2):
            time_copy(k, q).wait_send()
        for i in range(3):
            store(i, q).wait()


def per_device(field_a, field_b, pairs, signs):
    fy, fx, ix, iy, fz, iz = tables()
    a = jnp.transpose(field_a[0], (1, 0, 2))
    b = jnp.transpose(field_b[0], (1, 0, 2))
    dma = pltpu.SemaphoreType.DMA
    outs = pl.pallas_call(
        whole_kernel,
        out_shape=[jax.ShapeDtypeStruct((3, 4, 18432), F32)] * 3,
        in_specs=[ANY, ANY, SMEM, SMEM] + [VMEM] * 6,
        out_specs=[ANY] * 3,
        scratch_shapes=[
            pltpu.VMEM((2, 3, 8, 18432), F32),
            pltpu.VMEM((2, 3, 4, 384, 128), F32),
            pltpu.VMEM((3, 3, PEERS * 24, 128), F32),
            pltpu.VMEM((3, 3, CELLS * 24, 128), F32),
            pltpu.VMEM((3, 3, PEERS * 24, 128), F32),
            pltpu.VMEM((8, 192, 256), F32),
            pltpu.VMEM((4, 192, 128), F32),
            pltpu.VMEM((256, 8, 128), F32),
            pltpu.VMEM((2, 24, PEERS, 128), F32),
            pltpu.VMEM((PEERS * 8, 128), F32),
            pltpu.VMEM((2, PEERS * 24, 128), F32),
            pltpu.VMEM((CELLS * 8, 128), F32),
            pltpu.VMEM((2, CELLS * 24, 128), F32),
            pltpu.VMEM((PEERS * 8, 128), F32),
            pltpu.VMEM((2, PEERS * 24, 128), F32),
            pltpu.VMEM((3, 4, 192, 128), F32),
            pltpu.VMEM((3, 192, 384), F32),
            pltpu.VMEM((2, 3, 192, 384), F32),
            pltpu.VMEM((3, 3, 4, 18432), F32),
            dma((2, 3)),
            dma((3, 3)),
            dma((3, 3, 3)),
            dma((3, 3)),
            dma((3, 3)),
            dma((2,)),
            dma((2, 3)),
            dma((3,)),
            dma((3,)),
            dma((2, 3)),
            dma((2, 3)),
            dma((2, 3)),
            dma((2, 3)),
        ],
        compiler_params=pltpu.CompilerParams(vmem_limit_bytes=60_000_000, collective_id=0, has_side_effects=True),
        name="whole",
    )(a, b, jnp.transpose(pairs, (0, 2, 1)), signs, fz, fy, fx, ix, iy, iz)
    return tuple(jnp.transpose(out, (1, 0, 2))[None] for out in outs)


def solution(mesh):
    spec = P("tm", None, "space", None)
    return jax.shard_map(
        per_device, mesh=mesh, in_specs=(spec, spec, P(), P()), out_specs=(spec,) * 3, check_vma=False
    )
```

```python
import math

import jax
import jax.numpy as jnp
import ml_dtypes
import numpy as np
from jax import lax
from jax.experimental import pallas as pl
from jax.experimental.pallas import tpu as pltpu
from jax.sharding import PartitionSpec as P

N = 96
PEERS = 32
CELLS = 16
MESH_ID = pl.DeviceIdType.MESH
F32 = jnp.float32
BF16 = jnp.bfloat16


def halves(table):
    high = table.astype(np.float32).astype(ml_dtypes.bfloat16)
    low = (table - high.astype(np.float64)).astype(np.float32).astype(ml_dtypes.bfloat16)
    return high, low


def trig(out_index, in_index):
    angle = (np.outer(out_index, in_index) % N) * (2.0 * math.pi / N)
    return np.cos(angle) / math.sqrt(N), np.sin(angle) / math.sqrt(N)


def left_table(out_index, in_index, in_parts, forward):
    cosines, sines = trig(out_index, in_index)
    turn = 1.0 if forward else -1.0
    real = np.where(in_parts[None, :] == 0, cosines, turn * sines)
    imag = np.where(in_parts[None, :] == 0, -turn * sines, cosines)
    return np.concatenate(halves(np.concatenate([real, imag], axis=0)), axis=0)


def plain_columns(index):
    return np.concatenate([index, index]), np.repeat([0, 1], N)


def tables():
    sites = np.arange(N)
    pairs_order = np.concatenate([2 * np.arange(48), 2 * np.arange(48) + 1])
    y_in = np.concatenate([2 * np.arange(48) + v for v in (0, 1) for _ in (0, 1)])
    y_parts = np.concatenate([np.full(48, part) for _ in (0, 1) for part in (0, 1)])
    dealt = np.concatenate([3 * np.arange(PEERS) + q for q in range(3)])
    forward_y = left_table(dealt, y_in, y_parts, True)
    forward_x = left_table(sites, *plain_columns(dealt), True)
    inverse_x = left_table(dealt, *plain_columns(sites), False)
    inverse_y = left_table(pairs_order, *plain_columns(dealt), False)
    cosines, sines = trig(sites, sites)
    forward_z = np.zeros((2, 256, 256))
    inverse_z = np.zeros((2, 256, 256))
    for v in (0, 1):
        rows = 64 * v
        forward_z[v, rows : rows + N, 0:N] = cosines
        forward_z[v, rows : rows + N, 128 : 128 + N] = -sines
        forward_z[v, rows + N : rows + 2 * N, 0:N] = sines
        forward_z[v, rows + N : rows + 2 * N, 128 : 128 + N] = cosines
        inverse_z[v, 0:N, rows : rows + N] = cosines
        inverse_z[v, 0:N, rows + N : rows + 2 * N] = sines
        inverse_z[v, 128 : 128 + N, rows : rows + N] = -sines
        inverse_z[v, 128 : 128 + N, rows + N : rows + 2 * N] = cosines
    fz = np.stack(halves(forward_z))
    iz = np.stack(halves(inverse_z))
    return forward_y, forward_x, inverse_x, inverse_y, fz, iz


def split(value):
    high = value.astype(BF16)
    return high, (value - high.astype(F32)).astype(BF16)


def mm(left, right):
    return jnp.dot(left, right, preferred_element_type=F32)


def apply_left(table, value):
    high, low = split(value)
    both = mm(table[...], high)
    return both[:192] + both[192:] + mm(table[0:192, :], low)


def apply_right(value, table, v):
    high, low = split(value)
    return mm(high, table[0, v]) + mm(low, table[0, v]) + mm(high, table[1, v])


def lanes(shape):
    return lax.broadcasted_iota(jnp.int32, shape, 1)


def depth_step(x_ref, x, fz, z_ref, slot):
    rows = jnp.concatenate([x_ref[x, :, 384 * u : 384 * u + 384] for u in range(48)], axis=0)
    for v in (0, 1):
        out = apply_right(rows[:, 128 * v : 128 * v + 256], fz, v)
        for part in (0, 1):
            z_ref[slot, x, 2 * v + part] = out[:, 128 * part : 128 * part + 128]


def rows_step(z_ref, fy, x, c, s_ref):
    sides = [
        jnp.concatenate([z_ref[f, x, i, pl.ds(c, 48, stride=8), :] for i in range(4)], axis=0)
        for f in (0, 1)
    ]
    out = apply_left(fy, jnp.concatenate(sides, axis=1))
    a_re, a_im = out[:96, :128], out[96:, :128]
    b_re, b_im = out[:96, 128:], out[96:, 128:]
    low = lanes((96, 128)) < 96
    packed = (
        jnp.where(low, a_re, pltpu.roll(b_im, 96, 1)),
        jnp.where(low, a_im, pltpu.roll(b_im, 64, 1)),
        jnp.where(low, b_re, pltpu.roll(b_im, 32, 1)),
    )
    for j in range(3):
        for q in range(3):
            s_ref[q, x, pl.ds(8 * j + c, PEERS, stride=24), :] = packed[j][32 * q : 32 * q + 32]


def columns_step(r_ref, q, fx, c, h_ref):
    got = [
        jnp.concatenate(
            [r_ref[q, x, pl.ds(8 * j + c, PEERS, stride=24), :] for x in range(3)], axis=0
        )
        for j in range(3)
    ]
    at = lanes((96, 128))
    b_im = jnp.where(
        at < 32, pltpu.roll(got[0], 32, 1), jnp.where(at < 64, pltpu.roll(got[1], 64, 1), pltpu.roll(got[2], 96, 1))
    )
    real = jnp.concatenate([got[0], got[2]], axis=1)
    imag = jnp.concatenate([got[1], b_im], axis=1)
    h_ref[c] = apply_left(fx, jnp.concatenate([real, imag], axis=0))


def weights_step(pairs_ref, signs_ref, w_ref):
    row = lax.broadcasted_iota(jnp.int32, (8, 128), 0)
    lane = lax.broadcasted_iota(jnp.int32, (8, 128), 1)

    @pl.loop(0, 4)
    def _(ch):
        total = jnp.zeros((8, 128), F32)
        for p in range(16):
            here = (row == pairs_ref[ch, 0, p]) & (lane == pairs_ref[ch, 1, p])
            total += jnp.where(here, signs_ref[ch, p].astype(F32), 0.0)
        for i in range(8):
            for j in range(8):
                w_ref[64 * ch + 8 * i + j] = jnp.broadcast_to(total[i : i + 1, j : j + 1], (8, 128))


def contract_step(w_ref, h_ref, m_ref):
    @pl.loop(0, 12)
    def _(row):
        re = pl.ds(pl.multiple_of(row * 8, 8), 8)
        im = pl.ds(pl.multiple_of(row * 8 + 96, 8), 8)
        b_re = [h_ref[j, re, 128:] for j in range(8)]
        b_im = [h_ref[j, im, 128:] for j in range(8)]

        @pl.loop(0, 4)
        def _(ch):
            sum_re, sum_im = jnp.zeros((8, 128), F32), jnp.zeros((8, 128), F32)
            for i in range(8):
                weight = w_ref[ch * 64 + i * 8]
                mix_re = weight * b_re[0]
                mix_im = weight * b_im[0]
                for j in range(1, 8):
                    weight = w_ref[ch * 64 + i * 8 + j]
                    mix_re += weight * b_re[j]
                    mix_im += weight * b_im[j]
                a_re, a_im = h_ref[i, re, :128], h_ref[i, im, :128]
                sum_re += a_re * mix_re + a_im * mix_im
                sum_im += a_im * mix_re - a_re * mix_im
            m_ref[ch, re, :] = sum_re
            m_ref[ch, im, :] = sum_im


def columns_back_step(m_ref, ix, q, cs0_ref, cs_ref, k_ref):
    at = lanes((32, 128))
    for pair in range(2):
        value = jnp.concatenate([m_ref[2 * pair], m_ref[2 * pair + 1]], axis=1)
        out = apply_left(ix, value)

        def block(k, part, x):
            first = 96 * part + 32 * x
            return out[first : first + 32, 128 * k : 128 * k + 128]

        @pl.when(q == 0)
        def _():
            for k in range(2):
                for part in range(2):
                    row = 4 * part + 2 * pair + k
                    got = [block(k, part, x) for x in range(3)]
                    for x in range(3):
                        k_ref[0, 8 * x + row] = pltpu.roll(got[x], 96, 1)
                        k_ref[1, 8 * x + row] = pltpu.roll(got[x], 64, 1)
                    cs0_ref[pl.ds(row, PEERS, stride=8), :] = jnp.where(
                        at < 32, pltpu.roll(got[0], 64, 1), jnp.where(at < 64, pltpu.roll(got[1], 96, 1), got[2])
                    )

        @pl.when(q > 0)
        def _():
            for k in range(2):
                for part in range(2):
                    for x in range(3):
                        row = 8 * x + 4 * part + 2 * pair + k
                        cs_ref[q - 1, pl.ds(row, PEERS, stride=24), :] = jnp.where(
                            at < 96, block(k, part, x), k_ref[q - 1, row]
                        )


def rows_back_step(cr0_ref, cr_ref, iy, x, pair, g_ref):
    at = lanes((32, 128))
    sides = []
    for k in range(2):
        ch = 2 * pair + k
        parts = []
        for part in range(2):
            own = cr0_ref[pl.ds(4 * part + ch, PEERS, stride=8), :]
            second, third = (cr_ref[i, pl.ds(8 * x + 4 * part + ch, PEERS, stride=24), :] for i in range(2))
            first = jnp.where(
                at < 32,
                pltpu.roll(second, 32, 1),
                jnp.where(at < 64, pltpu.roll(third, 64, 1), pltpu.roll(own, (64 - 32 * x) % 128, 1)),
            )
            parts += [first, second, third]
        sides.append(jnp.concatenate(parts, axis=0))
    out = apply_left(iy, jnp.concatenate(sides, axis=1))
    for k in range(2):
        ch = 2 * pair + k
        for part in range(2):
            for v in range(2):
                first = 96 * part + 48 * v
                g_ref[x, 2 * v + part, pl.ds(ch, 48, stride=4), :] = out[
                    first : first + 48, 128 * k : 128 * k + 128
                ]


def depth_back_step(g_ref, iz, x, o_ref):
    outs = []
    for v in (0, 1):
        value = jnp.concatenate([g_ref[x, 2 * v], g_ref[x, 2 * v + 1]], axis=1)
        value = jnp.where(lax.rem(lanes((192, 256)), 128) < 96, value, 0.0)
        outs.append(apply_right(value, iz, v))
    o_ref[x, :, 0:128] = outs[0][:, :128]
    o_ref[x, :, 128:256] = outs[0][:, 128:] + outs[1][:, :128]
    o_ref[x, :, 256:384] = outs[1][:, 128:]


VMEM = pl.BlockSpec(memory_space=pltpu.VMEM)
SMEM = pl.BlockSpec(memory_space=pltpu.SMEM)
ANY = pl.BlockSpec(memory_space=pl.ANY)


def difference_step(o_ref, n_ref, out_ref, x):
    for pair in range(24):
        rows = pl.ds(pair * 8, 8)
        now, later, earlier = o_ref[x, rows, :], n_ref[0, x, rows, :], n_ref[1, x, rows, :]
        first = later - now
        second = later - 2.0 * now + earlier
        for half in range(2):
            at = pl.ds(pair * 768 + half * 384, 384)
            out_ref[0, x, :, at] = now[4 * half : 4 * half + 4]
            out_ref[1, x, :, at] = first[4 * half : 4 * half + 4]
            out_ref[2, x, :, at] = second[4 * half : 4 * half + 4]


def differences_kernel(o_hbm, n_hbm, c_hbm, f_hbm, d_hbm, o_ref, n_ref, out_ref, in_sem, out_sem):
    def loads(x):
        return (
            pltpu.make_async_copy(o_hbm.at[x], o_ref.at[x], in_sem.at[0, x]),
            pltpu.make_async_copy(n_hbm.at[0, x], n_ref.at[0, x], in_sem.at[1, x]),
            pltpu.make_async_copy(n_hbm.at[1, x], n_ref.at[1, x], in_sem.at[2, x]),
        )

    def store(i, x):
        return pltpu.make_async_copy(out_ref.at[i, x], (c_hbm, f_hbm, d_hbm)[i].at[x], out_sem.at[i, x])

    for x in range(3):
        for copy in loads(x):
            copy.start()

    @pl.loop(0, 3)
    def _(x):
        for copy in loads(x):
            copy.wait()
        difference_step(o_ref, n_ref, out_ref, x)
        for i in range(3):
            store(i, x).start()

    for x in range(3):
        for i in range(3):
            store(i, x).wait()


def whole_kernel(
    a_hbm, b_hbm, pairs_ref, signs_ref, fz, fy, fx, ix, iy, iz,
    o_hbm, n_hbm,
    ab_ref, z_ref, s_ref, t_ref, r_ref, h_ref, m_ref, w_ref, k_ref, cs0_ref, cs_ref, ct0_ref, ct_ref, cr0_ref, cr_ref, g_ref, o_ref,
    in_sem, out_sem, own_sem, zs_sem, zr_sem, fs_sem, fr_sem, bs_sem, br_sem, cs_sem, cr_sem, ts_sem, tr_sem,
):
    me, tm = lax.axis_index("space"), lax.axis_index("tm")
    near = (lax.rem(tm + 7, 8), lax.rem(tm + 1, 8))
    half, cell = me // CELLS, lax.rem(me, CELLS)
    partner = lax.rem(me + CELLS, PEERS)
    far = (1 - half) * CELLS

    def cell_of(k):
        along_x = lax.rem(cell // 4 + k // 4, 4)
        along_y = lax.rem(lax.rem(cell, 4) + lax.rem(k, 4), 4)
        return 4 * along_x + along_y

    def rows(first, count=1):
        return pl.ds(pl.multiple_of(first * 24, 8), count * 24)

    def remote(src, dst, send, recv, space, time=None):
        return pltpu.make_async_remote_copy(
            src_ref=src,
            dst_ref=dst,
            send_sem=send,
            recv_sem=recv,
            device_id=(tm if time is None else time, space),
            device_id_type=MESH_ID,
        )

    def each_cell(act):
        @pl.loop(1, CELLS)
        def _(k):
            act(cell_of(k))

    def load(f, x):
        return pltpu.make_async_copy((a_hbm, b_hbm)[f].at[x], ab_ref.at[f, x], in_sem.at[f, x])

    for x in range(3):
        for f in range(2):
            load(f, x).start()
    barrier = pltpu.get_barrier_semaphore()
    pl.semaphore_signal(barrier, inc=1, device_id=(tm, partner), device_id_type=MESH_ID)
    each_cell(
        lambda to: pl.semaphore_signal(
            barrier, inc=1, device_id=(tm, half * CELLS + to), device_id_type=MESH_ID
        )
    )
    for k in range(2):
        pl.semaphore_signal(barrier, inc=1, device_id=(near[k], me), device_id_type=MESH_ID)

    def cross(q, x):
        return remote(s_ref.at[q, x, rows(far, CELLS)], t_ref.at[q, x], zs_sem.at[q, x], zr_sem.at[q, x], partner)

    def spread(q, x, to):
        at = half * CELLS + to
        return remote(s_ref.at[q, x, rows(at)], r_ref.at[q, x, rows(me)], fs_sem.at[0], fr_sem.at[0, q], at)

    def relay(q, x, to):
        at = half * CELLS + to
        return remote(t_ref.at[q, x, rows(to)], r_ref.at[q, x, rows(partner)], fs_sem.at[1], fr_sem.at[1, q], at)

    def keep(q, x):
        return pltpu.make_async_copy(s_ref.at[q, x, rows(me)], r_ref.at[q, x, rows(me)], own_sem.at[0, q, x])

    def keep_relay(q, x):
        return pltpu.make_async_copy(t_ref.at[q, x, rows(cell)], r_ref.at[q, x, rows(partner)], own_sem.at[1, q, x])

    def group(refs, g, first, count=1):
        size = 24 if g else 8
        at = pl.ds(pl.multiple_of(first * size, 8), count * size)
        return refs[1].at[g - 1, at] if g else refs[0].at[at]

    made, passed, final = (cs0_ref, cs_ref), (ct0_ref, ct_ref), (cr0_ref, cr_ref)

    def cross_back(g):
        return remote(group(made, g, far, CELLS), group(passed, g, 0, CELLS), bs_sem.at[g], br_sem.at[g], partner)

    def spread_back(g, to):
        at = half * CELLS + to
        return remote(group(made, g, at), group(final, g, me), cs_sem.at[0, g], cr_sem.at[0, g], at)

    def relay_back(g, to):
        at = half * CELLS + to
        return remote(group(passed, g, to), group(final, g, partner), cs_sem.at[1, g], cr_sem.at[1, g], at)

    def all_back(i, g):
        some = group(final, g, 0, CELLS - 1)
        return remote(some, some, cs_sem.at[i, g], cr_sem.at[i, g], partner)

    def keep_back(g):
        return pltpu.make_async_copy(group(made, g, me), group(final, g, me), own_sem.at[2, g, 0])

    def keep_relay_back(g):
        return pltpu.make_async_copy(group(passed, g, cell), group(final, g, partner), own_sem.at[2, g, 1])

    def send_back(g):
        cross_back(g).start()
        each_cell(lambda to: spread_back(g, to).start())
        keep_back(g).start()

    def time_copy(k, x):
        return remote(o_ref.at[x], n_hbm.at[k, x], ts_sem.at[k, x], tr_sem.at[k, x], me, near[k])

    def store(x):
        return pltpu.make_async_copy(o_ref.at[x], o_hbm.at[x], out_sem.at[x])

    def send(q, x):
        cross(q, x).start()
        each_cell(lambda to: spread(q, x, to).start())
        keep(q, x).start()

    @pl.loop(0, 3)
    def _(x):
        for f in range(2):
            load(f, x).wait()
            depth_step(ab_ref.at[f], x, fz, z_ref, f)

        @pl.loop(0, 8, unroll=4)
        def _(c):
            rows_step(z_ref, fy, x, c, s_ref)

        @pl.when(x == 0)
        def _():
            pl.semaphore_wait(barrier, CELLS + 2)

        send(0, x)

    @pl.loop(0, 6)
    def _(i):
        send(1 + i // 3, lax.rem(i, 3))

    every = pl.ds(0, 24 * (CELLS - 1))
    weights_step(pairs_ref, signs_ref, w_ref)

    @pl.loop(0, 3)
    def _(q):
        @pl.loop(0, 3)
        def _(x):
            cross(q, x).wait_recv()
            each_cell(lambda to: relay(q, x, to).start())
            keep_relay(q, x).start()
            keep(q, x).wait()

        for i in range(2):
            remote(r_ref.at[q, :, every], r_ref.at[q, :, every], fs_sem.at[i], fr_sem.at[i, q], partner).wait_recv()

        @pl.loop(0, 3)
        def _(x):
            keep_relay(q, x).wait()

        @pl.loop(0, 8, unroll=4)
        def _(c):
            columns_step(r_ref, q, fx, c, h_ref)

        contract_step(w_ref, h_ref, m_ref)
        columns_back_step(m_ref, ix, q, cs0_ref, cs_ref, k_ref)
        for g in range(3):

            @pl.when(q == g)
            def _():
                send_back(g)

    for g in range(3):
        cross_back(g).wait_recv()
        each_cell(lambda to: relay_back(g, to).start())
        keep_relay_back(g).start()
        keep_back(g).wait()
    for g in range(3):
        for i in range(2):
            all_back(i, g).wait_recv()
        keep_relay_back(g).wait()

    for x in range(3):
        for pair in range(2):
            rows_back_step(cr0_ref, cr_ref, iy, x, pair, g_ref)
        depth_back_step(g_ref, iz, x, o_ref)
        for k in range(2):
            time_copy(k, x).start()
        store(x).start()

    for i in range(2):
        remote(s_ref.at[:, :, every], s_ref.at[:, :, every], fs_sem.at[i], fr_sem.at[i, 0], partner).wait_send()
        for g in range(3):
            all_back(i, g).wait_send()
    for g in range(3):
        cross_back(g).wait_send()

    @pl.loop(0, 3)
    def _(q):
        for x in range(3):
            cross(q, x).wait_send()
        for k in range(2):
            time_copy(k, q).wait_send()
            time_copy(k, q).wait_recv()
        store(q).wait()


def per_device(field_a, field_b, pairs, signs):
    fy, fx, ix, iy, fz, iz = tables()
    a = jnp.transpose(field_a[0], (1, 0, 2))
    b = jnp.transpose(field_b[0], (1, 0, 2))
    dma = pltpu.SemaphoreType.DMA
    own, others = pl.pallas_call(
        whole_kernel,
        out_shape=[jax.ShapeDtypeStruct((3, 192, 384), F32), jax.ShapeDtypeStruct((2, 3, 192, 384), F32)],
        in_specs=[ANY, ANY, SMEM, SMEM] + [VMEM] * 6,
        out_specs=[ANY] * 2,
        scratch_shapes=[
            pltpu.VMEM((2, 3, 8, 18432), F32),
            pltpu.VMEM((2, 3, 4, 384, 128), F32),
            pltpu.VMEM((3, 3, PEERS * 24, 128), F32),
            pltpu.VMEM((3, 3, CELLS * 24, 128), F32),
            pltpu.VMEM((3, 3, PEERS * 24, 128), F32),
            pltpu.VMEM((8, 192, 256), F32),
            pltpu.VMEM((4, 192, 128), F32),
            pltpu.VMEM((256, 8, 128), F32),
            pltpu.VMEM((2, 24, PEERS, 128), F32),
            pltpu.VMEM((PEERS * 8, 128), F32),
            pltpu.VMEM((2, PEERS * 24, 128), F32),
            pltpu.VMEM((CELLS * 8, 128), F32),
            pltpu.VMEM((2, CELLS * 24, 128), F32),
            pltpu.VMEM((PEERS * 8, 128), F32),
            pltpu.VMEM((2, PEERS * 24, 128), F32),
            pltpu.VMEM((3, 4, 192, 128), F32),
            pltpu.VMEM((3, 192, 384), F32),
            dma((2, 3)),
            dma((3,)),
            dma((3, 3, 3)),
            dma((3, 3)),
            dma((3, 3)),
            dma((2,)),
            dma((2, 3)),
            dma((3,)),
            dma((3,)),
            dma((2, 3)),
            dma((2, 3)),
            dma((2, 3)),
            dma((2, 3)),
        ],
        compiler_params=pltpu.CompilerParams(vmem_limit_bytes=60_000_000, collective_id=0, has_side_effects=True),
        name="whole",
    )(a, b, jnp.transpose(pairs, (0, 2, 1)), signs, fz, fy, fx, ix, iy, iz)
    outs = pl.pallas_call(
        differences_kernel,
        out_shape=[jax.ShapeDtypeStruct((3, 4, 18432), F32)] * 3,
        in_specs=[ANY] * 2,
        out_specs=[ANY] * 3,
        scratch_shapes=[
            pltpu.VMEM((3, 192, 384), F32),
            pltpu.VMEM((2, 3, 192, 384), F32),
            pltpu.VMEM((3, 3, 4, 18432), F32),
            dma((3, 3)),
            dma((3, 3)),
        ],
        compiler_params=pltpu.CompilerParams(vmem_limit_bytes=62_000_000),
        name="differences",
    )(own, others)
    return tuple(jnp.transpose(out, (1, 0, 2))[None] for out in outs)


def solution(mesh):
    spec = P("tm", None, "space", None)
    return jax.shard_map(
        per_device, mesh=mesh, in_specs=(spec, spec, P(), P()), out_specs=(spec,) * 3, check_vma=False
    )
```

```python
import math

import jax
import jax.numpy as jnp
import ml_dtypes
import numpy as np
from jax import lax
from jax.experimental import pallas as pl
from jax.experimental.pallas import tpu as pltpu
from jax.sharding import PartitionSpec as P

N = 96
PEERS = 32
CELLS = 16
MESH_ID = pl.DeviceIdType.MESH
F32 = jnp.float32
BF16 = jnp.bfloat16


def halves(table):
    high = table.astype(np.float32).astype(ml_dtypes.bfloat16)
    low = (table - high.astype(np.float64)).astype(np.float32).astype(ml_dtypes.bfloat16)
    return high, low


def trig(out_index, in_index):
    angle = (np.outer(out_index, in_index) % N) * (2.0 * math.pi / N)
    return np.cos(angle) / math.sqrt(N), np.sin(angle) / math.sqrt(N)


def left_table(out_index, in_index, in_parts, forward):
    cosines, sines = trig(out_index, in_index)
    turn = 1.0 if forward else -1.0
    real = np.where(in_parts[None, :] == 0, cosines, turn * sines)
    imag = np.where(in_parts[None, :] == 0, -turn * sines, cosines)
    return np.concatenate(halves(np.concatenate([real, imag], axis=0)), axis=0)


def plain_columns(index):
    return np.concatenate([index, index]), np.repeat([0, 1], N)


def tables():
    sites = np.arange(N)
    pairs_order = np.concatenate([2 * np.arange(48), 2 * np.arange(48) + 1])
    y_in = np.concatenate([2 * np.arange(48) + v for v in (0, 1) for _ in (0, 1)])
    y_parts = np.concatenate([np.full(48, part) for _ in (0, 1) for part in (0, 1)])
    dealt = np.concatenate([3 * np.arange(PEERS) + q for q in range(3)])
    forward_y = left_table(dealt, y_in, y_parts, True)
    forward_x = left_table(sites, *plain_columns(dealt), True)
    inverse_x = left_table(dealt, *plain_columns(sites), False)
    inverse_y = left_table(pairs_order, *plain_columns(dealt), False)
    cosines, sines = trig(sites, sites)
    forward_z = np.zeros((2, 256, 256))
    inverse_z = np.zeros((2, 256, 256))
    for v in (0, 1):
        rows = 64 * v
        forward_z[v, rows : rows + N, 0:N] = cosines
        forward_z[v, rows : rows + N, 128 : 128 + N] = -sines
        forward_z[v, rows + N : rows + 2 * N, 0:N] = sines
        forward_z[v, rows + N : rows + 2 * N, 128 : 128 + N] = cosines
        inverse_z[v, 0:N, rows : rows + N] = cosines
        inverse_z[v, 0:N, rows + N : rows + 2 * N] = sines
        inverse_z[v, 128 : 128 + N, rows : rows + N] = -sines
        inverse_z[v, 128 : 128 + N, rows + N : rows + 2 * N] = cosines
    fz = np.stack(halves(forward_z))
    iz = np.stack(halves(inverse_z))
    return forward_y, forward_x, inverse_x, inverse_y, fz, iz


def split(value):
    high = value.astype(BF16)
    return high, (value - high.astype(F32)).astype(BF16)


def mm(left, right):
    return jnp.dot(left, right, preferred_element_type=F32)


def apply_left(table, value):
    high, low = split(value)
    both = mm(table[...], high)
    return both[:192] + both[192:] + mm(table[0:192, :], low)


def apply_right(value, table, v):
    high, low = split(value)
    return mm(high, table[0, v]) + mm(low, table[0, v]) + mm(high, table[1, v])


def lanes(shape):
    return lax.broadcasted_iota(jnp.int32, shape, 1)


def depth_step(x_ref, x, fz, z_ref, slot):
    rows = jnp.concatenate([x_ref[x, :, 384 * u : 384 * u + 384] for u in range(48)], axis=0)
    for v in (0, 1):
        out = apply_right(rows[:, 128 * v : 128 * v + 256], fz, v)
        for part in (0, 1):
            z_ref[slot, x, 2 * v + part] = out[:, 128 * part : 128 * part + 128]


def rows_step(z_ref, fy, x, c, s_ref):
    sides = [
        jnp.concatenate([z_ref[f, x, i, pl.ds(c, 48, stride=8), :] for i in range(4)], axis=0)
        for f in (0, 1)
    ]
    out = apply_left(fy, jnp.concatenate(sides, axis=1))
    a_re, a_im = out[:96, :128], out[96:, :128]
    b_re, b_im = out[:96, 128:], out[96:, 128:]
    low = lanes((96, 128)) < 96
    packed = (
        jnp.where(low, a_re, pltpu.roll(b_im, 96, 1)),
        jnp.where(low, a_im, pltpu.roll(b_im, 64, 1)),
        jnp.where(low, b_re, pltpu.roll(b_im, 32, 1)),
    )
    for j in range(3):
        for q in range(3):
            s_ref[q, x, pl.ds(8 * j + c, PEERS, stride=24), :] = packed[j][32 * q : 32 * q + 32]


def columns_step(r_ref, q, fx, c, h_ref):
    got = [
        jnp.concatenate(
            [r_ref[q, x, pl.ds(8 * j + c, PEERS, stride=24), :] for x in range(3)], axis=0
        )
        for j in range(3)
    ]
    at = lanes((96, 128))
    b_im = jnp.where(
        at < 32, pltpu.roll(got[0], 32, 1), jnp.where(at < 64, pltpu.roll(got[1], 64, 1), pltpu.roll(got[2], 96, 1))
    )
    real = jnp.concatenate([got[0], got[2]], axis=1)
    imag = jnp.concatenate([got[1], b_im], axis=1)
    h_ref[c] = apply_left(fx, jnp.concatenate([real, imag], axis=0))


def weights_step(pairs_ref, signs_ref, w_ref):
    row = lax.broadcasted_iota(jnp.int32, (8, 128), 0)
    lane = lax.broadcasted_iota(jnp.int32, (8, 128), 1)

    @pl.loop(0, 4)
    def _(ch):
        total = jnp.zeros((8, 128), F32)
        for p in range(16):
            here = (row == pairs_ref[ch, 0, p]) & (lane == pairs_ref[ch, 1, p])
            total += jnp.where(here, signs_ref[ch, p].astype(F32), 0.0)
        for i in range(8):
            for j in range(8):
                w_ref[64 * ch + 8 * i + j] = jnp.broadcast_to(total[i : i + 1, j : j + 1], (8, 128))


def contract_step(w_ref, h_ref, m_ref):
    @pl.loop(0, 12)
    def _(row):
        re = pl.ds(pl.multiple_of(row * 8, 8), 8)
        im = pl.ds(pl.multiple_of(row * 8 + 96, 8), 8)
        b_re = [h_ref[j, re, 128:] for j in range(8)]
        b_im = [h_ref[j, im, 128:] for j in range(8)]

        @pl.loop(0, 4)
        def _(ch):
            sum_re, sum_im = jnp.zeros((8, 128), F32), jnp.zeros((8, 128), F32)
            for i in range(8):
                weight = w_ref[ch * 64 + i * 8]
                mix_re = weight * b_re[0]
                mix_im = weight * b_im[0]
                for j in range(1, 8):
                    weight = w_ref[ch * 64 + i * 8 + j]
                    mix_re += weight * b_re[j]
                    mix_im += weight * b_im[j]
                a_re, a_im = h_ref[i, re, :128], h_ref[i, im, :128]
                sum_re += a_re * mix_re + a_im * mix_im
                sum_im += a_im * mix_re - a_re * mix_im
            m_ref[ch, re, :] = sum_re
            m_ref[ch, im, :] = sum_im


def columns_back_step(m_ref, ix, q, cs0_ref, cs_ref, k_ref):
    at = lanes((32, 128))
    for pair in range(2):
        value = jnp.concatenate([m_ref[2 * pair], m_ref[2 * pair + 1]], axis=1)
        out = apply_left(ix, value)

        def block(k, part, x):
            first = 96 * part + 32 * x
            return out[first : first + 32, 128 * k : 128 * k + 128]

        @pl.when(q == 0)
        def _():
            for k in range(2):
                for part in range(2):
                    row = 4 * part + 2 * pair + k
                    got = [block(k, part, x) for x in range(3)]
                    for x in range(3):
                        k_ref[0, 8 * x + row] = pltpu.roll(got[x], 96, 1)
                        k_ref[1, 8 * x + row] = pltpu.roll(got[x], 64, 1)
                    cs0_ref[pl.ds(row, PEERS, stride=8), :] = jnp.where(
                        at < 32, pltpu.roll(got[0], 64, 1), jnp.where(at < 64, pltpu.roll(got[1], 96, 1), got[2])
                    )

        @pl.when(q > 0)
        def _():
            for k in range(2):
                for part in range(2):
                    for x in range(3):
                        row = 8 * x + 4 * part + 2 * pair + k
                        cs_ref[q - 1, pl.ds(row, PEERS, stride=24), :] = jnp.where(
                            at < 96, block(k, part, x), k_ref[q - 1, row]
                        )


def rows_back_step(cr0_ref, cr_ref, iy, x, pair, g_ref):
    at = lanes((32, 128))
    sides = []
    for k in range(2):
        ch = 2 * pair + k
        parts = []
        for part in range(2):
            own = cr0_ref[pl.ds(4 * part + ch, PEERS, stride=8), :]
            second, third = (cr_ref[i, pl.ds(8 * x + 4 * part + ch, PEERS, stride=24), :] for i in range(2))
            first = jnp.where(
                at < 32,
                pltpu.roll(second, 32, 1),
                jnp.where(at < 64, pltpu.roll(third, 64, 1), pltpu.roll(own, (64 - 32 * x) % 128, 1)),
            )
            parts += [first, second, third]
        sides.append(jnp.concatenate(parts, axis=0))
    out = apply_left(iy, jnp.concatenate(sides, axis=1))
    for k in range(2):
        ch = 2 * pair + k
        for part in range(2):
            for v in range(2):
                first = 96 * part + 48 * v
                g_ref[x, 2 * v + part, pl.ds(ch, 48, stride=4), :] = out[
                    first : first + 48, 128 * k : 128 * k + 128
                ]


def depth_back_step(g_ref, iz, x, o_ref):
    outs = []
    for v in (0, 1):
        value = jnp.concatenate([g_ref[x, 2 * v], g_ref[x, 2 * v + 1]], axis=1)
        value = jnp.where(lax.rem(lanes((192, 256)), 128) < 96, value, 0.0)
        outs.append(apply_right(value, iz, v))
    o_ref[x, :, 0:128] = outs[0][:, :128]
    o_ref[x, :, 128:256] = outs[0][:, 128:] + outs[1][:, :128]
    o_ref[x, :, 256:384] = outs[1][:, 128:]


VMEM = pl.BlockSpec(memory_space=pltpu.VMEM)
SMEM = pl.BlockSpec(memory_space=pltpu.SMEM)
ANY = pl.BlockSpec(memory_space=pl.ANY)


def difference_step(o_ref, n_ref, out_ref, x):
    for pair in range(24):
        rows = pl.ds(pair * 8, 8)
        now, later, earlier = o_ref[x, rows, :], n_ref[0, x, rows, :], n_ref[1, x, rows, :]
        first = later - now
        second = later - 2.0 * now + earlier
        for half in range(2):
            at = pl.ds(pair * 768 + half * 384, 384)
            out_ref[0, x, :, at] = now[4 * half : 4 * half + 4]
            out_ref[1, x, :, at] = first[4 * half : 4 * half + 4]
            out_ref[2, x, :, at] = second[4 * half : 4 * half + 4]


def differences_kernel(o_hbm, n_hbm, c_hbm, f_hbm, d_hbm, o_ref, n_ref, out_ref, in_sem, out_sem):
    def loads(x):
        return (
            pltpu.make_async_copy(o_hbm.at[x], o_ref.at[x], in_sem.at[0, x]),
            pltpu.make_async_copy(n_hbm.at[0, x], n_ref.at[0, x], in_sem.at[1, x]),
            pltpu.make_async_copy(n_hbm.at[1, x], n_ref.at[1, x], in_sem.at[2, x]),
        )

    def store(i, x):
        return pltpu.make_async_copy(out_ref.at[i, x], (c_hbm, f_hbm, d_hbm)[i].at[x], out_sem.at[i, x])

    for x in range(3):
        for copy in loads(x):
            copy.start()

    @pl.loop(0, 3)
    def _(x):
        for copy in loads(x):
            copy.wait()
        difference_step(o_ref, n_ref, out_ref, x)
        for i in range(3):
            store(i, x).start()

    for x in range(3):
        for i in range(3):
            store(i, x).wait()


def whole_kernel(
    a_hbm, b_hbm, pairs_ref, signs_ref, fz_hbm, fy_hbm, fx_hbm, ix_hbm, iy_hbm, iz_hbm,
    o_hbm, n_hbm,
    ab_ref, z_ref, s_ref, t_ref, r_ref, h_ref, m_ref, w_ref, k_ref, cs0_ref, cs_ref, ct0_ref, ct_ref, cr0_ref, cr_ref, et0_ref, et_ref, ef0_ref, ef_ref, g_ref, o_ref, e_ref, fz, fy, fx, ix, iy, iz,
    table_sem, in_sem, out_sem, own_sem, zs_sem, zr_sem, fs_sem, fr_sem, bs_sem, br_sem, cs_sem, cr_sem, ts_sem, tr_sem, es_sem, er_sem, fs2_sem, fr2_sem, ek_sem,
):
    me, tm = lax.axis_index("space"), lax.axis_index("tm")
    near = (lax.rem(tm + 7, 8), lax.rem(tm + 1, 8))
    half, cell = me // CELLS, lax.rem(me, CELLS)
    partner = lax.rem(me + CELLS, PEERS)
    far = (1 - half) * CELLS
    at_end = lax.rem(tm, 7) == 0
    other = 7 - tm

    def cell_of(k):
        along_x = lax.rem(cell // 4 + k // 4, 4)
        along_y = lax.rem(lax.rem(cell, 4) + lax.rem(k, 4), 4)
        return 4 * along_x + along_y

    def rows(first, count=1):
        return pl.ds(pl.multiple_of(first * 24, 8), count * 24)

    def remote(src, dst, send, recv, space, time=None):
        return pltpu.make_async_remote_copy(
            src_ref=src,
            dst_ref=dst,
            send_sem=send,
            recv_sem=recv,
            device_id=(tm if time is None else time, space),
            device_id_type=MESH_ID,
        )

    def each_cell(act):
        @pl.loop(1, CELLS)
        def _(k):
            act(cell_of(k))

    def load(f, x):
        return pltpu.make_async_copy((a_hbm, b_hbm)[f].at[x], ab_ref.at[f, x], in_sem.at[f, x])

    tables_hbm = (fz_hbm, fy_hbm, fx_hbm, ix_hbm, iy_hbm, iz_hbm)
    loads = [
        pltpu.make_async_copy(src, dst, table_sem.at[i])
        for i, (src, dst) in enumerate(zip(tables_hbm, (fz, fy, fx, ix, iy, iz)))
    ]
    for f in range(2):
        load(f, 0).start()
    for copy in loads[:2]:
        copy.start()
    for x in range(1, 3):
        for f in range(2):
            load(f, x).start()
    for copy in loads[2:]:
        copy.start()
    barrier = pltpu.get_barrier_semaphore()
    pl.semaphore_signal(barrier, inc=1, device_id=(tm, partner), device_id_type=MESH_ID)
    each_cell(
        lambda to: pl.semaphore_signal(
            barrier, inc=1, device_id=(tm, half * CELLS + to), device_id_type=MESH_ID
        )
    )
    for k in range(2):
        pl.semaphore_signal(barrier, inc=1, device_id=(near[k], me), device_id_type=MESH_ID)

    @pl.when(at_end)
    def _():
        pl.semaphore_signal(barrier, inc=1, device_id=(other, partner), device_id_type=MESH_ID)

    def cross(q, x):
        return remote(s_ref.at[q, x, rows(far, CELLS)], t_ref.at[q, x], zs_sem.at[q, x], zr_sem.at[q, x], partner)

    def spread(q, x, to):
        at = half * CELLS + to
        return remote(s_ref.at[q, x, rows(at)], r_ref.at[q, x, rows(me)], fs_sem.at[0], fr_sem.at[0, q], at)

    def relay(q, x, to):
        at = half * CELLS + to
        return remote(t_ref.at[q, x, rows(to)], r_ref.at[q, x, rows(partner)], fs_sem.at[1], fr_sem.at[1, q], at)

    def keep(q, x):
        return pltpu.make_async_copy(s_ref.at[q, x, rows(me)], r_ref.at[q, x, rows(me)], own_sem.at[0, q, x])

    def keep_relay(q, x):
        return pltpu.make_async_copy(t_ref.at[q, x, rows(cell)], r_ref.at[q, x, rows(partner)], own_sem.at[1, q, x])

    def group(refs, g, first, count=1):
        size = 24 if g else 8
        at = pl.ds(pl.multiple_of(first * size, 8), count * size)
        return refs[1].at[g - 1, at] if g else refs[0].at[at]

    made, passed, final = (cs0_ref, cs_ref), (ct0_ref, ct_ref), (cr0_ref, cr_ref)

    def cross_back(g):
        return remote(group(made, g, far, CELLS), group(passed, g, 0, CELLS), bs_sem.at[g], br_sem.at[g], partner)

    def spread_back(g, to):
        at = half * CELLS + to
        return remote(group(made, g, at), group(final, g, me), cs_sem.at[0, g], cr_sem.at[0, g], at)

    def relay_back(g, to):
        at = half * CELLS + to
        return remote(group(passed, g, to), group(final, g, partner), cs_sem.at[1, g], cr_sem.at[1, g], at)

    def all_back(i, g):
        some = group(final, g, 0, CELLS - 1)
        return remote(some, some, cs_sem.at[i, g], cr_sem.at[i, g], partner)

    def keep_back(g):
        return pltpu.make_async_copy(group(made, g, me), group(final, g, me), own_sem.at[2, g, 0])

    def keep_relay_back(g):
        return pltpu.make_async_copy(group(passed, g, cell), group(final, g, partner), own_sem.at[2, g, 1])

    holders = (me, partner)
    ends = [(et0_ref.at[i], et_ref.at[i]) for i in range(2)]
    end_final = (ef0_ref, ef_ref)

    def cross_end(g, i):
        first = (half * CELLS, far)[i]
        src, dst = group(made, g, first, CELLS), group(ends[i], g, 0, CELLS)
        return remote(src, dst, es_sem.at[i, g], er_sem.at[i, g], holders[i], other)

    def relay_end(g, i, to):
        src, dst = group(ends[i], g, to), group(end_final, g, holders[i])
        return remote(src, dst, fs2_sem.at[i, g], fr2_sem.at[i, g], half * CELLS + to)

    def all_end(i, g):
        some = group(end_final, g, 0, CELLS - 1)
        return remote(some, some, fs2_sem.at[i, g], fr2_sem.at[i, g], partner)

    def keep_end(g, i):
        return pltpu.make_async_copy(group(ends[i], g, cell), group(end_final, g, holders[i]), ek_sem.at[i, g])

    def store_end(x):
        return pltpu.make_async_copy(e_ref.at[x], n_hbm.at[1 - tm // 7, x], ek_sem.at[2, x])

    def send_back(g):
        cross_back(g).start()
        each_cell(lambda to: spread_back(g, to).start())
        keep_back(g).start()

    def time_copy(k, x):
        return remote(o_ref.at[x], n_hbm.at[k, x], ts_sem.at[k, x], tr_sem.at[k, x], me, near[k])

    def store(x):
        return pltpu.make_async_copy(o_ref.at[x], o_hbm.at[x], out_sem.at[x])

    def send(q, x):
        cross(q, x).start()
        each_cell(lambda to: spread(q, x, to).start())
        keep(q, x).start()

    for copy in loads[:2]:
        copy.wait()

    @pl.loop(0, 3)
    def _(x):
        for f in range(2):
            load(f, x).wait()
            depth_step(ab_ref.at[f], x, fz, z_ref, f)

        @pl.loop(0, 8, unroll=4)
        def _(c):
            rows_step(z_ref, fy, x, c, s_ref)

        @pl.when((x == 0) & at_end)
        def _():
            pl.semaphore_wait(barrier, CELLS + 3)

        @pl.when((x == 0) & jnp.logical_not(at_end))
        def _():
            pl.semaphore_wait(barrier, CELLS + 2)

        send(0, x)

    @pl.loop(0, 6)
    def _(i):
        send(1 + i // 3, lax.rem(i, 3))

    every = pl.ds(0, 24 * (CELLS - 1))
    weights_step(pairs_ref, signs_ref, w_ref)
    for copy in loads[2:]:
        copy.wait()

    @pl.loop(0, 3)
    def _(q):
        @pl.loop(0, 3)
        def _(x):
            cross(q, x).wait_recv()
            each_cell(lambda to: relay(q, x, to).start())
            keep_relay(q, x).start()
            keep(q, x).wait()

        for i in range(2):
            remote(r_ref.at[q, :, every], r_ref.at[q, :, every], fs_sem.at[i], fr_sem.at[i, q], partner).wait_recv()

        @pl.loop(0, 3)
        def _(x):
            keep_relay(q, x).wait()

        @pl.loop(0, 8, unroll=4)
        def _(c):
            columns_step(r_ref, q, fx, c, h_ref)

        contract_step(w_ref, h_ref, m_ref)
        columns_back_step(m_ref, ix, q, cs0_ref, cs_ref, k_ref)
        for g in range(3):

            @pl.when(q == g)
            def _():
                send_back(g)

    for g in range(3):
        cross_back(g).wait_recv()
        each_cell(lambda to: relay_back(g, to).start())
        keep_relay_back(g).start()
        keep_back(g).wait()
    for g in range(3):
        for i in range(2):
            all_back(i, g).wait_recv()
        keep_relay_back(g).wait()

    for x in range(3):
        for pair in range(2):
            rows_back_step(cr0_ref, cr_ref, iy, x, pair, g_ref)
        depth_back_step(g_ref, iz, x, o_ref)

        @pl.when(tm > 0)
        def _():
            time_copy(0, x).start()

        @pl.when(tm < 7)
        def _():
            time_copy(1, x).start()

        store(x).start()

    @pl.when(at_end)
    def _():
        for g in range(3):
            for i in (1, 0):
                cross_end(g, i).start()

    @pl.when(at_end)
    def _():
        for g in range(3):
            for i in (1, 0):
                cross_end(g, i).wait_recv()
                each_cell(lambda to: relay_end(g, i, to).start())
                keep_end(g, i).start()
        for g in range(3):
            for i in range(2):
                all_end(i, g).wait_recv()
                keep_end(g, i).wait()
        for x in range(3):
            for pair in range(2):
                rows_back_step(ef0_ref, ef_ref, iy, x, pair, g_ref)
            depth_back_step(g_ref, iz, x, e_ref)
            store_end(x).start()
        for x in range(3):
            store_end(x).wait()
        for g in range(3):
            for i in range(2):
                all_end(i, g).wait_send()
                cross_end(g, i).wait_send()

    for i in range(2):
        remote(s_ref.at[:, :, every], s_ref.at[:, :, every], fs_sem.at[i], fr_sem.at[i, 0], partner).wait_send()
        for g in range(3):
            all_back(i, g).wait_send()
    for g in range(3):
        cross_back(g).wait_send()

    @pl.loop(0, 3)
    def _(q):
        for x in range(3):
            cross(q, x).wait_send()
        store(q).wait()

        @pl.when(tm > 0)
        def _():
            time_copy(0, q).wait_send()
            time_copy(1, q).wait_recv()

        @pl.when(tm < 7)
        def _():
            time_copy(1, q).wait_send()
            time_copy(0, q).wait_recv()


def per_device(field_a, field_b, pairs, signs):
    fy, fx, ix, iy, fz, iz = tables()
    a = jnp.transpose(field_a[0], (1, 0, 2))
    b = jnp.transpose(field_b[0], (1, 0, 2))
    dma = pltpu.SemaphoreType.DMA
    own, others = pl.pallas_call(
        whole_kernel,
        out_shape=[jax.ShapeDtypeStruct((3, 192, 384), F32), jax.ShapeDtypeStruct((2, 3, 192, 384), F32)],
        in_specs=[ANY, ANY, SMEM, SMEM] + [ANY] * 6,
        out_specs=[ANY] * 2,
        scratch_shapes=[
            pltpu.VMEM((2, 3, 8, 18432), F32),
            pltpu.VMEM((2, 3, 4, 384, 128), F32),
            pltpu.VMEM((3, 3, PEERS * 24, 128), F32),
            pltpu.VMEM((3, 3, CELLS * 24, 128), F32),
            pltpu.VMEM((3, 3, PEERS * 24, 128), F32),
            pltpu.VMEM((8, 192, 256), F32),
            pltpu.VMEM((4, 192, 128), F32),
            pltpu.VMEM((256, 8, 128), F32),
            pltpu.VMEM((2, 24, PEERS, 128), F32),
            pltpu.VMEM((PEERS * 8, 128), F32),
            pltpu.VMEM((2, PEERS * 24, 128), F32),
            pltpu.VMEM((CELLS * 8, 128), F32),
            pltpu.VMEM((2, CELLS * 24, 128), F32),
            pltpu.VMEM((PEERS * 8, 128), F32),
            pltpu.VMEM((2, PEERS * 24, 128), F32),
            pltpu.VMEM((2, CELLS * 8, 128), F32),
            pltpu.VMEM((2, 2, CELLS * 24, 128), F32),
            pltpu.VMEM((PEERS * 8, 128), F32),
            pltpu.VMEM((2, PEERS * 24, 128), F32),
            pltpu.VMEM((3, 4, 192, 128), F32),
            pltpu.VMEM((3, 192, 384), F32),
            pltpu.VMEM((3, 192, 384), F32),
            pltpu.VMEM(fz.shape, BF16),
            pltpu.VMEM(fy.shape, BF16),
            pltpu.VMEM(fx.shape, BF16),
            pltpu.VMEM(ix.shape, BF16),
            pltpu.VMEM(iy.shape, BF16),
            pltpu.VMEM(iz.shape, BF16),
            dma((6,)),
            dma((2, 3)),
            dma((3,)),
            dma((3, 3, 3)),
            dma((3, 3)),
            dma((3, 3)),
            dma((2,)),
            dma((2, 3)),
            dma((3,)),
            dma((3,)),
            dma((2, 3)),
            dma((2, 3)),
            dma((2, 3)),
            dma((2, 3)),
            dma((2, 3)),
            dma((2, 3)),
            dma((2, 3)),
            dma((2, 3)),
            dma((3, 3)),
        ],
        compiler_params=pltpu.CompilerParams(vmem_limit_bytes=60_000_000, collective_id=0, has_side_effects=True),
        name="whole",
    )(a, b, jnp.transpose(pairs, (0, 2, 1)), signs, fz, fy, fx, ix, iy, iz)
    outs = pl.pallas_call(
        differences_kernel,
        out_shape=[jax.ShapeDtypeStruct((3, 4, 18432), F32)] * 3,
        in_specs=[ANY] * 2,
        out_specs=[ANY] * 3,
        scratch_shapes=[
            pltpu.VMEM((3, 192, 384), F32),
            pltpu.VMEM((2, 3, 192, 384), F32),
            pltpu.VMEM((3, 3, 4, 18432), F32),
            dma((3, 3)),
            dma((3, 3)),
        ],
        compiler_params=pltpu.CompilerParams(vmem_limit_bytes=62_000_000),
        name="differences",
    )(own, others)
    return tuple(jnp.transpose(out, (1, 0, 2))[None] for out in outs)


def solution(mesh):
    spec = P("tm", None, "space", None)
    return jax.shard_map(
        per_device, mesh=mesh, in_specs=(spec, spec, P(), P()), out_specs=(spec,) * 3, check_vma=False
    )
```

```python
import math

import jax
import jax.numpy as jnp
import ml_dtypes
import numpy as np
from jax import lax
from jax.experimental import pallas as pl
from jax.experimental.pallas import tpu as pltpu
from jax.sharding import PartitionSpec as P

N = 96
PEERS = 32
CELLS = 16
MESH_ID = pl.DeviceIdType.MESH
F32 = jnp.float32
BF16 = jnp.bfloat16


def halves(table):
    high = table.astype(np.float32).astype(ml_dtypes.bfloat16)
    low = (table - high.astype(np.float64)).astype(np.float32).astype(ml_dtypes.bfloat16)
    return high, low


def trig(out_index, in_index):
    angle = (np.outer(out_index, in_index) % N) * (2.0 * math.pi / N)
    return np.cos(angle) / math.sqrt(N), np.sin(angle) / math.sqrt(N)


def left_table(out_index, in_index, in_parts, forward):
    cosines, sines = trig(out_index, in_index)
    turn = 1.0 if forward else -1.0
    real = np.where(in_parts[None, :] == 0, cosines, turn * sines)
    imag = np.where(in_parts[None, :] == 0, -turn * sines, cosines)
    return np.concatenate(halves(np.concatenate([real, imag], axis=0)), axis=0)


def plain_columns(index):
    return np.concatenate([index, index]), np.repeat([0, 1], N)


def tables():
    sites = np.arange(N)
    pairs_order = np.concatenate([2 * np.arange(48), 2 * np.arange(48) + 1])
    y_in = np.concatenate([2 * np.arange(48) + v for v in (0, 1) for _ in (0, 1)])
    y_parts = np.concatenate([np.full(48, part) for _ in (0, 1) for part in (0, 1)])
    dealt = np.concatenate([3 * np.arange(PEERS) + q for q in range(3)])
    forward_y = left_table(dealt, y_in, y_parts, True)
    forward_x = left_table(sites, *plain_columns(dealt), True)
    inverse_x = left_table(dealt, *plain_columns(sites), False)
    inverse_y = left_table(pairs_order, *plain_columns(dealt), False)
    cosines, sines = trig(sites, sites)
    forward_z = np.zeros((2, 256, 256))
    inverse_z = np.zeros((2, 256, 256))
    for v in (0, 1):
        rows = 64 * v
        forward_z[v, rows : rows + N, 0:N] = cosines
        forward_z[v, rows : rows + N, 128 : 128 + N] = -sines
        forward_z[v, rows + N : rows + 2 * N, 0:N] = sines
        forward_z[v, rows + N : rows + 2 * N, 128 : 128 + N] = cosines
        inverse_z[v, 0:N, rows : rows + N] = cosines
        inverse_z[v, 0:N, rows + N : rows + 2 * N] = sines
        inverse_z[v, 128 : 128 + N, rows : rows + N] = -sines
        inverse_z[v, 128 : 128 + N, rows + N : rows + 2 * N] = cosines
    fz = np.stack(halves(forward_z))
    iz = np.stack(halves(inverse_z))
    return forward_y, forward_x, inverse_x, inverse_y, fz, iz


def split(value):
    high = value.astype(BF16)
    return high, (value - high.astype(F32)).astype(BF16)


def mm(left, right):
    return jnp.dot(left, right, preferred_element_type=F32)


def apply_left(table, value):
    high, low = split(value)
    both = mm(table[...], high)
    return both[:192] + both[192:] + mm(table[0:192, :], low)


def apply_right(value, table, v):
    high, low = split(value)
    return mm(high, table[0, v]) + mm(low, table[0, v]) + mm(high, table[1, v])


def lanes(shape):
    return lax.broadcasted_iota(jnp.int32, shape, 1)


def depth_step(x_ref, x, fz, z_ref, slot):
    rows = jnp.concatenate([x_ref[x, :, 384 * u : 384 * u + 384] for u in range(48)], axis=0)
    for v in (0, 1):
        out = apply_right(rows[:, 128 * v : 128 * v + 256], fz, v)
        for part in (0, 1):
            z_ref[slot, x, 2 * v + part] = out[:, 128 * part : 128 * part + 128]


def rows_step(z_ref, fy, x, c, s_ref):
    sides = [
        jnp.concatenate([z_ref[f, x, i, pl.ds(c, 48, stride=8), :] for i in range(4)], axis=0)
        for f in (0, 1)
    ]
    out = apply_left(fy, jnp.concatenate(sides, axis=1))
    a_re, a_im = out[:96, :128], out[96:, :128]
    b_re, b_im = out[:96, 128:], out[96:, 128:]
    low = lanes((96, 128)) < 96
    packed = (
        jnp.where(low, a_re, pltpu.roll(b_im, 96, 1)),
        jnp.where(low, a_im, pltpu.roll(b_im, 64, 1)),
        jnp.where(low, b_re, pltpu.roll(b_im, 32, 1)),
    )
    for j in range(3):
        for q in range(3):
            s_ref[q, x, pl.ds(8 * j + c, PEERS, stride=24), :] = packed[j][32 * q : 32 * q + 32]


def columns_step(r_ref, q, fx, c, h_ref):
    got = [
        jnp.concatenate(
            [r_ref[q, x, pl.ds(8 * j + c, PEERS, stride=24), :] for x in range(3)], axis=0
        )
        for j in range(3)
    ]
    at = lanes((96, 128))
    b_im = jnp.where(
        at < 32, pltpu.roll(got[0], 32, 1), jnp.where(at < 64, pltpu.roll(got[1], 64, 1), pltpu.roll(got[2], 96, 1))
    )
    real = jnp.concatenate([got[0], got[2]], axis=1)
    imag = jnp.concatenate([got[1], b_im], axis=1)
    h_ref[c] = apply_left(fx, jnp.concatenate([real, imag], axis=0))


def weights_step(pairs_ref, signs_ref, w_ref):
    row = lax.broadcasted_iota(jnp.int32, (8, 128), 0)
    lane = lax.broadcasted_iota(jnp.int32, (8, 128), 1)

    @pl.loop(0, 4)
    def _(ch):
        total = jnp.zeros((8, 128), F32)
        for p in range(16):
            here = (row == pairs_ref[ch, 0, p]) & (lane == pairs_ref[ch, 1, p])
            total += jnp.where(here, signs_ref[ch, p].astype(F32), 0.0)
        for i in range(8):
            for j in range(8):
                w_ref[64 * ch + 8 * i + j] = jnp.broadcast_to(total[i : i + 1, j : j + 1], (8, 128))


def contract_step(w_ref, h_ref, m_ref):
    @pl.loop(0, 12)
    def _(row):
        re = pl.ds(pl.multiple_of(row * 8, 8), 8)
        im = pl.ds(pl.multiple_of(row * 8 + 96, 8), 8)
        b_re = [h_ref[j, re, 128:] for j in range(8)]
        b_im = [h_ref[j, im, 128:] for j in range(8)]

        @pl.loop(0, 4)
        def _(ch):
            sum_re, sum_im = jnp.zeros((8, 128), F32), jnp.zeros((8, 128), F32)
            for i in range(8):
                weight = w_ref[ch * 64 + i * 8]
                mix_re = weight * b_re[0]
                mix_im = weight * b_im[0]
                for j in range(1, 8):
                    weight = w_ref[ch * 64 + i * 8 + j]
                    mix_re += weight * b_re[j]
                    mix_im += weight * b_im[j]
                a_re, a_im = h_ref[i, re, :128], h_ref[i, im, :128]
                sum_re += a_re * mix_re + a_im * mix_im
                sum_im += a_im * mix_re - a_re * mix_im
            m_ref[ch, re, :] = sum_re
            m_ref[ch, im, :] = sum_im


def columns_back_step(m_ref, ix, q, cs0_ref, cs_ref, k_ref):
    at = lanes((32, 128))
    for pair in range(2):
        value = jnp.concatenate([m_ref[2 * pair], m_ref[2 * pair + 1]], axis=1)
        out = apply_left(ix, value)

        def block(k, part, x):
            first = 96 * part + 32 * x
            return out[first : first + 32, 128 * k : 128 * k + 128]

        @pl.when(q == 0)
        def _():
            for k in range(2):
                for part in range(2):
                    row = 4 * part + 2 * pair + k
                    got = [block(k, part, x) for x in range(3)]
                    for x in range(3):
                        k_ref[0, 8 * x + row] = pltpu.roll(got[x], 96, 1)
                        k_ref[1, 8 * x + row] = pltpu.roll(got[x], 64, 1)
                    cs0_ref[pl.ds(row, PEERS, stride=8), :] = jnp.where(
                        at < 32, pltpu.roll(got[0], 64, 1), jnp.where(at < 64, pltpu.roll(got[1], 96, 1), got[2])
                    )

        @pl.when(q > 0)
        def _():
            for k in range(2):
                for part in range(2):
                    for x in range(3):
                        row = 8 * x + 4 * part + 2 * pair + k
                        cs_ref[q - 1, pl.ds(row, PEERS, stride=24), :] = jnp.where(
                            at < 96, block(k, part, x), k_ref[q - 1, row]
                        )


def rows_back_step(cr0_ref, cr_ref, iy, x, pair, g_ref):
    at = lanes((32, 128))
    sides = []
    for k in range(2):
        ch = 2 * pair + k
        parts = []
        for part in range(2):
            own = cr0_ref[pl.ds(4 * part + ch, PEERS, stride=8), :]
            second, third = (cr_ref[i, pl.ds(8 * x + 4 * part + ch, PEERS, stride=24), :] for i in range(2))
            first = jnp.where(
                at < 32,
                pltpu.roll(second, 32, 1),
                jnp.where(at < 64, pltpu.roll(third, 64, 1), pltpu.roll(own, (64 - 32 * x) % 128, 1)),
            )
            parts += [first, second, third]
        sides.append(jnp.concatenate(parts, axis=0))
    out = apply_left(iy, jnp.concatenate(sides, axis=1))
    for k in range(2):
        ch = 2 * pair + k
        for part in range(2):
            for v in range(2):
                first = 96 * part + 48 * v
                g_ref[x, 2 * v + part, pl.ds(ch, 48, stride=4), :] = out[
                    first : first + 48, 128 * k : 128 * k + 128
                ]


def depth_back_step(g_ref, iz, x, o_ref):
    outs = []
    for v in (0, 1):
        value = jnp.concatenate([g_ref[x, 2 * v], g_ref[x, 2 * v + 1]], axis=1)
        value = jnp.where(lax.rem(lanes((192, 256)), 128) < 96, value, 0.0)
        outs.append(apply_right(value, iz, v))
    o_ref[x, :, 0:128] = outs[0][:, :128]
    o_ref[x, :, 128:256] = outs[0][:, 128:] + outs[1][:, :128]
    o_ref[x, :, 256:384] = outs[1][:, 128:]


VMEM = pl.BlockSpec(memory_space=pltpu.VMEM)
SMEM = pl.BlockSpec(memory_space=pltpu.SMEM)
ANY = pl.BlockSpec(memory_space=pl.ANY)


def difference_step(o_ref, n_ref, out_ref, x):
    for pair in range(24):
        rows = pl.ds(pair * 8, 8)
        now, later, earlier = o_ref[x, rows, :], n_ref[0, x, rows, :], n_ref[1, x, rows, :]
        first = later - now
        second = later - 2.0 * now + earlier
        for half in range(2):
            at = pl.ds(pair * 768 + half * 384, 384)
            out_ref[0, x, :, at] = now[4 * half : 4 * half + 4]
            out_ref[1, x, :, at] = first[4 * half : 4 * half + 4]
            out_ref[2, x, :, at] = second[4 * half : 4 * half + 4]


def differences_kernel(o_hbm, n_hbm, c_hbm, f_hbm, d_hbm, o_ref, n_ref, out_ref, in_sem, out_sem):
    def loads(x):
        return (
            pltpu.make_async_copy(o_hbm.at[x], o_ref.at[x], in_sem.at[0, x]),
            pltpu.make_async_copy(n_hbm.at[0, x], n_ref.at[0, x], in_sem.at[1, x]),
            pltpu.make_async_copy(n_hbm.at[1, x], n_ref.at[1, x], in_sem.at[2, x]),
        )

    def store(i, x):
        return pltpu.make_async_copy(out_ref.at[i, x], (c_hbm, f_hbm, d_hbm)[i].at[x], out_sem.at[i, x])

    for x in range(3):
        for copy in loads(x):
            copy.start()

    @pl.loop(0, 3)
    def _(x):
        for copy in loads(x):
            copy.wait()
        difference_step(o_ref, n_ref, out_ref, x)
        for i in range(3):
            store(i, x).start()

    for x in range(3):
        for i in range(3):
            store(i, x).wait()


def whole_kernel(
    a_hbm, b_hbm, pairs_ref, signs_ref, fz_hbm, fy_hbm, fx_hbm, ix_hbm, iy_hbm, iz_hbm,
    o_hbm, n_hbm,
    ab_ref, z_ref, s_ref, t_ref, r_ref, h_ref, m_ref, w_ref, k_ref, cs0_ref, cs_ref, ct0_ref, ct_ref, cr0_ref, cr_ref, et0_ref, et_ref, ef0_ref, ef_ref, g_ref, o_ref, e_ref, fz, fy, fx, ix, iy, iz,
    table_sem, in_sem, out_sem, own_sem, zs_sem, zr_sem, fs_sem, fr_sem, bs_sem, br_sem, cs_sem, cr_sem, ts_sem, tr_sem, es_sem, er_sem, fs2_sem, fr2_sem, ek_sem,
):
    me, tm = lax.axis_index("space"), lax.axis_index("tm")
    near = (lax.rem(tm + 7, 8), lax.rem(tm + 1, 8))
    half, cell = me // CELLS, lax.rem(me, CELLS)
    partner = lax.rem(me + CELLS, PEERS)
    far = (1 - half) * CELLS
    at_end = lax.rem(tm, 7) == 0
    other = 7 - tm

    def cell_of(k):
        along_x = lax.rem(cell // 4 + k // 4, 4)
        along_y = lax.rem(lax.rem(cell, 4) + lax.rem(k, 4), 4)
        return 4 * along_x + along_y

    def rows(first, count=1):
        return pl.ds(pl.multiple_of(first * 24, 8), count * 24)

    def remote(src, dst, send, recv, space, time=None):
        return pltpu.make_async_remote_copy(
            src_ref=src,
            dst_ref=dst,
            send_sem=send,
            recv_sem=recv,
            device_id=(tm if time is None else time, space),
            device_id_type=MESH_ID,
        )

    def each_cell(act):
        @pl.loop(1, CELLS)
        def _(k):
            act(cell_of(k))

    def load(f, x):
        return pltpu.make_async_copy((a_hbm, b_hbm)[f].at[x], ab_ref.at[f, x], in_sem.at[f, x])

    tables_hbm = (fz_hbm, fy_hbm, fx_hbm, ix_hbm, iy_hbm, iz_hbm)
    loads = [
        pltpu.make_async_copy(src, dst, table_sem.at[i])
        for i, (src, dst) in enumerate(zip(tables_hbm, (fz, fy, fx, ix, iy, iz)))
    ]
    for f in range(2):
        load(f, 0).start()
    for copy in loads[:2]:
        copy.start()
    for x in range(1, 3):
        for f in range(2):
            load(f, x).start()
    for copy in loads[2:]:
        copy.start()
    barrier = pltpu.get_barrier_semaphore()
    pl.semaphore_signal(barrier, inc=1, device_id=(tm, partner), device_id_type=MESH_ID)
    each_cell(
        lambda to: pl.semaphore_signal(
            barrier, inc=1, device_id=(tm, half * CELLS + to), device_id_type=MESH_ID
        )
    )
    for k in range(2):
        pl.semaphore_signal(barrier, inc=1, device_id=(near[k], me), device_id_type=MESH_ID)

    @pl.when(at_end)
    def _():
        pl.semaphore_signal(barrier, inc=1, device_id=(other, partner), device_id_type=MESH_ID)

    def cross(q, x):
        return remote(s_ref.at[q, x, rows(far, CELLS)], t_ref.at[q, x], zs_sem.at[q, x], zr_sem.at[q, x], partner)

    def spread(q, x, to):
        at = half * CELLS + to
        return remote(s_ref.at[q, x, rows(at)], r_ref.at[q, x, rows(me)], fs_sem.at[0], fr_sem.at[0, q], at)

    def relay(q, x, to):
        at = half * CELLS + to
        return remote(t_ref.at[q, x, rows(to)], r_ref.at[q, x, rows(partner)], fs_sem.at[1], fr_sem.at[1, q], at)

    def keep(q, x):
        return pltpu.make_async_copy(s_ref.at[q, x, rows(me)], r_ref.at[q, x, rows(me)], own_sem.at[0, q, x])

    def keep_relay(q, x):
        return pltpu.make_async_copy(t_ref.at[q, x, rows(cell)], r_ref.at[q, x, rows(partner)], own_sem.at[1, q, x])

    def group(refs, g, first, count=1):
        size = 24 if g else 8
        at = pl.ds(pl.multiple_of(first * size, 8), count * size)
        return refs[1].at[g - 1, at] if g else refs[0].at[at]

    made, passed, final = (cs0_ref, cs_ref), (ct0_ref, ct_ref), (cr0_ref, cr_ref)

    def cross_back(g):
        return remote(group(made, g, far, CELLS), group(passed, g, 0, CELLS), bs_sem.at[g], br_sem.at[g], partner)

    def spread_back(g, to):
        at = half * CELLS + to
        return remote(group(made, g, at), group(final, g, me), cs_sem.at[0, g], cr_sem.at[0, g], at)

    def relay_back(g, to):
        at = half * CELLS + to
        return remote(group(passed, g, to), group(final, g, partner), cs_sem.at[1, g], cr_sem.at[1, g], at)

    def all_back(i, g):
        some = group(final, g, 0, CELLS - 1)
        return remote(some, some, cs_sem.at[i, g], cr_sem.at[i, g], partner)

    def keep_back(g):
        return pltpu.make_async_copy(group(made, g, me), group(final, g, me), own_sem.at[2, g, 0])

    def keep_relay_back(g):
        return pltpu.make_async_copy(group(passed, g, cell), group(final, g, partner), own_sem.at[2, g, 1])

    holders = (me, partner)
    ends = [(et0_ref.at[i], et_ref.at[i]) for i in range(2)]
    end_final = (ef0_ref, ef_ref)

    def cross_end(g, i):
        first = (half * CELLS, far)[i]
        src, dst = group(made, g, first, CELLS), group(ends[i], g, 0, CELLS)
        return remote(src, dst, es_sem.at[i, g], er_sem.at[i, g], holders[i], other)

    def relay_end(g, i, to):
        src, dst = group(ends[i], g, to), group(end_final, g, holders[i])
        return remote(src, dst, fs2_sem.at[i, g], fr2_sem.at[i, g], half * CELLS + to)

    def all_end(i, g):
        some = group(end_final, g, 0, CELLS - 1)
        return remote(some, some, fs2_sem.at[i, g], fr2_sem.at[i, g], partner)

    def keep_end(g, i):
        return pltpu.make_async_copy(group(ends[i], g, cell), group(end_final, g, holders[i]), ek_sem.at[i, g])

    def store_end(x):
        return pltpu.make_async_copy(e_ref.at[x], n_hbm.at[1 - tm // 7, x], ek_sem.at[2, x])

    def send_back(g):
        cross_back(g).start()
        each_cell(lambda to: spread_back(g, to).start())
        keep_back(g).start()

    def time_copy(k, x):
        return remote(o_ref.at[x], n_hbm.at[k, x], ts_sem.at[k, x], tr_sem.at[k, x], me, near[k])

    def store(x):
        return pltpu.make_async_copy(o_ref.at[x], o_hbm.at[x], out_sem.at[x])

    def send(q, x):
        cross(q, x).start()
        each_cell(lambda to: spread(q, x, to).start())
        keep(q, x).start()

    for copy in loads[:2]:
        copy.wait()

    @pl.loop(0, 3)
    def _(x):
        for f in range(2):
            load(f, x).wait()
            depth_step(ab_ref.at[f], x, fz, z_ref, f)

        @pl.loop(0, 8, unroll=4)
        def _(c):
            rows_step(z_ref, fy, x, c, s_ref)

        @pl.when((x == 0) & at_end)
        def _():
            pl.semaphore_wait(barrier, CELLS + 3)

        @pl.when((x == 0) & jnp.logical_not(at_end))
        def _():
            pl.semaphore_wait(barrier, CELLS + 2)

        send(0, x)

    @pl.loop(0, 6)
    def _(i):
        send(1 + i // 3, lax.rem(i, 3))

    every = pl.ds(0, 24 * (CELLS - 1))
    weights_step(pairs_ref, signs_ref, w_ref)
    for copy in loads[2:]:
        copy.wait()

    @pl.loop(0, 3)
    def _(q):
        @pl.loop(0, 3)
        def _(x):
            cross(q, x).wait_recv()
            each_cell(lambda to: relay(q, x, to).start())
            keep_relay(q, x).start()
            keep(q, x).wait()

        for i in range(2):
            remote(r_ref.at[q, :, every], r_ref.at[q, :, every], fs_sem.at[i], fr_sem.at[i, q], partner).wait_recv()

        @pl.loop(0, 3)
        def _(x):
            keep_relay(q, x).wait()

        @pl.loop(0, 8, unroll=4)
        def _(c):
            columns_step(r_ref, q, fx, c, h_ref)

        contract_step(w_ref, h_ref, m_ref)
        columns_back_step(m_ref, ix, q, cs0_ref, cs_ref, k_ref)
        for g in range(3):

            @pl.when(q == g)
            def _():
                send_back(g)

    @pl.when(at_end)
    def _():
        for g, i in ((0, 1), (1, 1), (2, 1)):
            cross_end(g, i).start()

    for g in range(3):
        cross_back(g).wait_recv()
        each_cell(lambda to: relay_back(g, to).start())
        keep_relay_back(g).start()
        keep_back(g).wait()
    for g in range(3):
        for i in range(2):
            all_back(i, g).wait_recv()
        keep_relay_back(g).wait()

    for x in range(3):
        for pair in range(2):
            rows_back_step(cr0_ref, cr_ref, iy, x, pair, g_ref)
        depth_back_step(g_ref, iz, x, o_ref)

        @pl.when(tm > 0)
        def _():
            time_copy(0, x).start()

        @pl.when(tm < 7)
        def _():
            time_copy(1, x).start()

        store(x).start()

    @pl.when(at_end)
    def _():
        for g, i in ((0, 0), (1, 0), (2, 0)):
            cross_end(g, i).start()

    @pl.when(at_end)
    def _():
        for i, g in [(i, g) for i in (1, 0) for g in range(3)]:
            cross_end(g, i).wait_recv()
            each_cell(lambda to: relay_end(g, i, to).start())
            keep_end(g, i).start()
        for g in range(3):
            for i in range(2):
                all_end(i, g).wait_recv()
                keep_end(g, i).wait()
        for x in range(3):
            for pair in range(2):
                rows_back_step(ef0_ref, ef_ref, iy, x, pair, g_ref)
            depth_back_step(g_ref, iz, x, e_ref)
            store_end(x).start()
        for x in range(3):
            store_end(x).wait()
        for g in range(3):
            for i in range(2):
                all_end(i, g).wait_send()
                cross_end(g, i).wait_send()

    for i in range(2):
        remote(s_ref.at[:, :, every], s_ref.at[:, :, every], fs_sem.at[i], fr_sem.at[i, 0], partner).wait_send()
        for g in range(3):
            all_back(i, g).wait_send()
    for g in range(3):
        cross_back(g).wait_send()

    @pl.loop(0, 3)
    def _(q):
        for x in range(3):
            cross(q, x).wait_send()
        store(q).wait()

        @pl.when(tm > 0)
        def _():
            time_copy(0, q).wait_send()
            time_copy(1, q).wait_recv()

        @pl.when(tm < 7)
        def _():
            time_copy(1, q).wait_send()
            time_copy(0, q).wait_recv()


def per_device(field_a, field_b, pairs, signs):
    fy, fx, ix, iy, fz, iz = tables()
    a = jnp.transpose(field_a[0], (1, 0, 2))
    b = jnp.transpose(field_b[0], (1, 0, 2))
    dma = pltpu.SemaphoreType.DMA
    own, others = pl.pallas_call(
        whole_kernel,
        out_shape=[jax.ShapeDtypeStruct((3, 192, 384), F32), jax.ShapeDtypeStruct((2, 3, 192, 384), F32)],
        in_specs=[ANY, ANY, SMEM, SMEM] + [ANY] * 6,
        out_specs=[ANY] * 2,
        scratch_shapes=[
            pltpu.VMEM((2, 3, 8, 18432), F32),
            pltpu.VMEM((2, 3, 4, 384, 128), F32),
            pltpu.VMEM((3, 3, PEERS * 24, 128), F32),
            pltpu.VMEM((3, 3, CELLS * 24, 128), F32),
            pltpu.VMEM((3, 3, PEERS * 24, 128), F32),
            pltpu.VMEM((8, 192, 256), F32),
            pltpu.VMEM((4, 192, 128), F32),
            pltpu.VMEM((256, 8, 128), F32),
            pltpu.VMEM((2, 24, PEERS, 128), F32),
            pltpu.VMEM((PEERS * 8, 128), F32),
            pltpu.VMEM((2, PEERS * 24, 128), F32),
            pltpu.VMEM((CELLS * 8, 128), F32),
            pltpu.VMEM((2, CELLS * 24, 128), F32),
            pltpu.VMEM((PEERS * 8, 128), F32),
            pltpu.VMEM((2, PEERS * 24, 128), F32),
            pltpu.VMEM((2, CELLS * 8, 128), F32),
            pltpu.VMEM((2, 2, CELLS * 24, 128), F32),
            pltpu.VMEM((PEERS * 8, 128), F32),
            pltpu.VMEM((2, PEERS * 24, 128), F32),
            pltpu.VMEM((3, 4, 192, 128), F32),
            pltpu.VMEM((3, 192, 384), F32),
            pltpu.VMEM((3, 192, 384), F32),
            pltpu.VMEM(fz.shape, BF16),
            pltpu.VMEM(fy.shape, BF16),
            pltpu.VMEM(fx.shape, BF16),
            pltpu.VMEM(ix.shape, BF16),
            pltpu.VMEM(iy.shape, BF16),
            pltpu.VMEM(iz.shape, BF16),
            dma((6,)),
            dma((2, 3)),
            dma((3,)),
            dma((3, 3, 3)),
            dma((3, 3)),
            dma((3, 3)),
            dma((2,)),
            dma((2, 3)),
            dma((3,)),
            dma((3,)),
            dma((2, 3)),
            dma((2, 3)),
            dma((2, 3)),
            dma((2, 3)),
            dma((2, 3)),
            dma((2, 3)),
            dma((2, 3)),
            dma((2, 3)),
            dma((3, 3)),
        ],
        compiler_params=pltpu.CompilerParams(vmem_limit_bytes=60_000_000, collective_id=0, has_side_effects=True),
        name="whole",
    )(a, b, jnp.transpose(pairs, (0, 2, 1)), signs, fz, fy, fx, ix, iy, iz)
    outs = pl.pallas_call(
        differences_kernel,
        out_shape=[jax.ShapeDtypeStruct((3, 4, 18432), F32)] * 3,
        in_specs=[ANY] * 2,
        out_specs=[ANY] * 3,
        scratch_shapes=[
            pltpu.VMEM((3, 192, 384), F32),
            pltpu.VMEM((2, 3, 192, 384), F32),
            pltpu.VMEM((3, 3, 4, 18432), F32),
            dma((3, 3)),
            dma((3, 3)),
        ],
        compiler_params=pltpu.CompilerParams(vmem_limit_bytes=62_000_000),
        name="differences",
    )(own, others)
    return tuple(jnp.transpose(out, (1, 0, 2))[None] for out in outs)


def solution(mesh):
    spec = P("tm", None, "space", None)
    return jax.shard_map(
        per_device, mesh=mesh, in_specs=(spec, spec, P(), P()), out_specs=(spec,) * 3, check_vma=False
    )
```

```python
import math

import jax
import jax.numpy as jnp
import ml_dtypes
import numpy as np
from jax import lax
from jax.experimental import pallas as pl
from jax.experimental.pallas import tpu as pltpu
from jax.sharding import PartitionSpec as P

N = 96
PEERS = 32
CELLS = 16
MESH_ID = pl.DeviceIdType.MESH
F32 = jnp.float32
BF16 = jnp.bfloat16


def halves(table):
    high = table.astype(np.float32).astype(ml_dtypes.bfloat16)
    low = (table - high.astype(np.float64)).astype(np.float32).astype(ml_dtypes.bfloat16)
    return high, low


def trig(out_index, in_index):
    angle = (np.outer(out_index, in_index) % N) * (2.0 * math.pi / N)
    return np.cos(angle) / math.sqrt(N), np.sin(angle) / math.sqrt(N)


def left_table(out_index, in_index, in_parts, forward):
    cosines, sines = trig(out_index, in_index)
    turn = 1.0 if forward else -1.0
    real = np.where(in_parts[None, :] == 0, cosines, turn * sines)
    imag = np.where(in_parts[None, :] == 0, -turn * sines, cosines)
    return np.concatenate(halves(np.concatenate([real, imag], axis=0)), axis=0)


def plain_columns(index):
    return np.concatenate([index, index]), np.repeat([0, 1], N)


def tables():
    sites = np.arange(N)
    pairs_order = np.concatenate([2 * np.arange(48), 2 * np.arange(48) + 1])
    y_in = np.concatenate([2 * np.arange(48) + v for v in (0, 1) for _ in (0, 1)])
    y_parts = np.concatenate([np.full(48, part) for _ in (0, 1) for part in (0, 1)])
    dealt = np.concatenate([3 * np.arange(PEERS) + q for q in range(3)])
    forward_y = left_table(dealt, y_in, y_parts, True)
    forward_x = left_table(sites, *plain_columns(dealt), True)
    inverse_x = left_table(dealt, *plain_columns(sites), False)
    inverse_y = left_table(pairs_order, *plain_columns(dealt), False)
    cosines, sines = trig(sites, sites)
    forward_z = np.zeros((2, 256, 256))
    inverse_z = np.zeros((2, 256, 256))
    for v in (0, 1):
        rows = 64 * v
        forward_z[v, rows : rows + N, 0:N] = cosines
        forward_z[v, rows : rows + N, 128 : 128 + N] = -sines
        forward_z[v, rows + N : rows + 2 * N, 0:N] = sines
        forward_z[v, rows + N : rows + 2 * N, 128 : 128 + N] = cosines
        inverse_z[v, 0:N, rows : rows + N] = cosines
        inverse_z[v, 0:N, rows + N : rows + 2 * N] = sines
        inverse_z[v, 128 : 128 + N, rows : rows + N] = -sines
        inverse_z[v, 128 : 128 + N, rows + N : rows + 2 * N] = cosines
    fz = np.stack(halves(forward_z))
    iz = np.stack(halves(inverse_z))
    return forward_y, forward_x, inverse_x, inverse_y, fz, iz


def split(value):
    high = value.astype(BF16)
    return high, (value - high.astype(F32)).astype(BF16)


def mm(left, right):
    return jnp.dot(left, right, preferred_element_type=F32)


def apply_left(table, value):
    high, low = split(value)
    both = mm(table[...], high)
    return both[:192] + both[192:] + mm(table[0:192, :], low)


def apply_right(value, table, v):
    high, low = split(value)
    return mm(high, table[0, v]) + mm(low, table[0, v]) + mm(high, table[1, v])


def lanes(shape):
    return lax.broadcasted_iota(jnp.int32, shape, 1)


def depth_step(x_ref, x, fz, z_ref, slot):
    rows = jnp.concatenate([x_ref[x, :, 384 * u : 384 * u + 384] for u in range(48)], axis=0)
    for v in (0, 1):
        out = apply_right(rows[:, 128 * v : 128 * v + 256], fz, v)
        for part in (0, 1):
            z_ref[slot, x, 2 * v + part] = out[:, 128 * part : 128 * part + 128]


def rows_step(z_ref, fy, x, c, s_ref):
    sides = [
        jnp.concatenate([z_ref[f, x, i, pl.ds(c, 48, stride=8), :] for i in range(4)], axis=0)
        for f in (0, 1)
    ]
    out = apply_left(fy, jnp.concatenate(sides, axis=1))
    a_re, a_im = out[:96, :128], out[96:, :128]
    b_re, b_im = out[:96, 128:], out[96:, 128:]
    low = lanes((96, 128)) < 96
    packed = (
        jnp.where(low, a_re, pltpu.roll(b_im, 96, 1)),
        jnp.where(low, a_im, pltpu.roll(b_im, 64, 1)),
        jnp.where(low, b_re, pltpu.roll(b_im, 32, 1)),
    )
    for j in range(3):
        for q in range(3):
            s_ref[q, x, pl.ds(8 * j + c, PEERS, stride=24), :] = packed[j][32 * q : 32 * q + 32]


def columns_step(r_ref, q, fx, c, h_ref):
    got = [
        jnp.concatenate(
            [r_ref[q, x, pl.ds(8 * j + c, PEERS, stride=24), :] for x in range(3)], axis=0
        )
        for j in range(3)
    ]
    at = lanes((96, 128))
    b_im = jnp.where(
        at < 32, pltpu.roll(got[0], 32, 1), jnp.where(at < 64, pltpu.roll(got[1], 64, 1), pltpu.roll(got[2], 96, 1))
    )
    real = jnp.concatenate([got[0], got[2]], axis=1)
    imag = jnp.concatenate([got[1], b_im], axis=1)
    h_ref[c] = apply_left(fx, jnp.concatenate([real, imag], axis=0))


def weights_step(pairs_ref, signs_ref, w_ref):
    row = lax.broadcasted_iota(jnp.int32, (8, 128), 0)
    lane = lax.broadcasted_iota(jnp.int32, (8, 128), 1)

    @pl.loop(0, 4)
    def _(ch):
        total = jnp.zeros((8, 128), F32)
        for p in range(16):
            here = (row == pairs_ref[ch, 0, p]) & (lane == pairs_ref[ch, 1, p])
            total += jnp.where(here, signs_ref[ch, p].astype(F32), 0.0)
        for i in range(8):
            for j in range(8):
                w_ref[64 * ch + 8 * i + j] = jnp.broadcast_to(total[i : i + 1, j : j + 1], (8, 128))


def contract_step(w_ref, h_ref, m_ref):
    @pl.loop(0, 12)
    def _(row):
        re = pl.ds(pl.multiple_of(row * 8, 8), 8)
        im = pl.ds(pl.multiple_of(row * 8 + 96, 8), 8)
        b_re = [h_ref[j, re, 128:] for j in range(8)]
        b_im = [h_ref[j, im, 128:] for j in range(8)]

        @pl.loop(0, 4, unroll=4)
        def _(ch):
            sum_re, sum_im = jnp.zeros((8, 128), F32), jnp.zeros((8, 128), F32)
            for i in range(8):
                weight = w_ref[ch * 64 + i * 8]
                mix_re = weight * b_re[0]
                mix_im = weight * b_im[0]
                for j in range(1, 8):
                    weight = w_ref[ch * 64 + i * 8 + j]
                    mix_re += weight * b_re[j]
                    mix_im += weight * b_im[j]
                a_re, a_im = h_ref[i, re, :128], h_ref[i, im, :128]
                sum_re += a_re * mix_re + a_im * mix_im
                sum_im += a_im * mix_re - a_re * mix_im
            m_ref[ch, re, :] = sum_re
            m_ref[ch, im, :] = sum_im


def columns_back_step(m_ref, ix, q, cs0_ref, cs_ref, k_ref):
    at = lanes((32, 128))
    for pair in range(2):
        value = jnp.concatenate([m_ref[2 * pair], m_ref[2 * pair + 1]], axis=1)
        out = apply_left(ix, value)

        def block(k, part, x):
            first = 96 * part + 32 * x
            return out[first : first + 32, 128 * k : 128 * k + 128]

        @pl.when(q == 0)
        def _():
            for k in range(2):
                for part in range(2):
                    row = 4 * part + 2 * pair + k
                    got = [block(k, part, x) for x in range(3)]
                    for x in range(3):
                        k_ref[0, 8 * x + row] = pltpu.roll(got[x], 96, 1)
                        k_ref[1, 8 * x + row] = pltpu.roll(got[x], 64, 1)
                    cs0_ref[pl.ds(row, PEERS, stride=8), :] = jnp.where(
                        at < 32, pltpu.roll(got[0], 64, 1), jnp.where(at < 64, pltpu.roll(got[1], 96, 1), got[2])
                    )

        @pl.when(q > 0)
        def _():
            for k in range(2):
                for part in range(2):
                    for x in range(3):
                        row = 8 * x + 4 * part + 2 * pair + k
                        cs_ref[q - 1, pl.ds(row, PEERS, stride=24), :] = jnp.where(
                            at < 96, block(k, part, x), k_ref[q - 1, row]
                        )


def rows_back_step(cr0_ref, cr_ref, iy, x, pair, g_ref):
    at = lanes((32, 128))
    sides = []
    for k in range(2):
        ch = 2 * pair + k
        parts = []
        for part in range(2):
            own = cr0_ref[pl.ds(4 * part + ch, PEERS, stride=8), :]
            second, third = (cr_ref[i, pl.ds(8 * x + 4 * part + ch, PEERS, stride=24), :] for i in range(2))
            first = jnp.where(
                at < 32,
                pltpu.roll(second, 32, 1),
                jnp.where(at < 64, pltpu.roll(third, 64, 1), pltpu.roll(own, (64 - 32 * x) % 128, 1)),
            )
            parts += [first, second, third]
        sides.append(jnp.concatenate(parts, axis=0))
    out = apply_left(iy, jnp.concatenate(sides, axis=1))
    for k in range(2):
        ch = 2 * pair + k
        for part in range(2):
            for v in range(2):
                first = 96 * part + 48 * v
                g_ref[x, 2 * v + part, pl.ds(ch, 48, stride=4), :] = out[
                    first : first + 48, 128 * k : 128 * k + 128
                ]


def depth_back_step(g_ref, iz, x, o_ref):
    outs = []
    for v in (0, 1):
        value = jnp.concatenate([g_ref[x, 2 * v], g_ref[x, 2 * v + 1]], axis=1)
        value = jnp.where(lax.rem(lanes((192, 256)), 128) < 96, value, 0.0)
        outs.append(apply_right(value, iz, v))
    o_ref[x, :, 0:128] = outs[0][:, :128]
    o_ref[x, :, 128:256] = outs[0][:, 128:] + outs[1][:, :128]
    o_ref[x, :, 256:384] = outs[1][:, 128:]


VMEM = pl.BlockSpec(memory_space=pltpu.VMEM)
SMEM = pl.BlockSpec(memory_space=pltpu.SMEM)
ANY = pl.BlockSpec(memory_space=pl.ANY)


def difference_step(o_ref, n_ref, out_ref, x, third):
    for pair in range(8):
        rows = pl.ds(pl.multiple_of(third * 64 + pair * 8, 8), 8)
        now, later, earlier = o_ref[x, rows, :], n_ref[0, x, rows, :], n_ref[1, x, rows, :]
        first = later - now
        second = later - 2.0 * now + earlier
        for half in range(2):
            at = pl.ds(pl.multiple_of(third * 6144 + pair * 768 + half * 384, 128), 384)
            out_ref[0, x, :, at] = now[4 * half : 4 * half + 4]
            out_ref[1, x, :, at] = first[4 * half : 4 * half + 4]
            out_ref[2, x, :, at] = second[4 * half : 4 * half + 4]


def differences_kernel(o_hbm, n_hbm, c_hbm, f_hbm, d_hbm, o_ref, n_ref, out_ref, in_sem, out_sem):
    def loads(i):
        x, rows = i // 3, pl.ds(pl.multiple_of(lax.rem(i, 3) * 64, 8), 64)
        return (
            pltpu.make_async_copy(o_hbm.at[x, rows], o_ref.at[x, rows], in_sem.at[0, i]),
            pltpu.make_async_copy(n_hbm.at[0, x, rows], n_ref.at[0, x, rows], in_sem.at[1, i]),
            pltpu.make_async_copy(n_hbm.at[1, x, rows], n_ref.at[1, x, rows], in_sem.at[2, i]),
        )

    def store(k, i):
        x, at = i // 3, pl.ds(pl.multiple_of(lax.rem(i, 3) * 6144, 128), 6144)
        out = (c_hbm, f_hbm, d_hbm)[k].at[x, :, at]
        return pltpu.make_async_copy(out_ref.at[k, x, :, at], out, out_sem.at[k, i])

    @pl.loop(0, 9)
    def _(i):
        for copy in loads(i):
            copy.start()

    @pl.loop(0, 9)
    def _(i):
        for copy in loads(i):
            copy.wait()
        difference_step(o_ref, n_ref, out_ref, i // 3, lax.rem(i, 3))
        for k in range(3):
            store(k, i).start()

    @pl.loop(0, 9)
    def _(i):
        for k in range(3):
            store(k, i).wait()


def whole_kernel(
    a_hbm, b_hbm, pairs_ref, signs_ref, fz_hbm, fy_hbm, fx_hbm, ix_hbm, iy_hbm, iz_hbm,
    o_hbm, n_hbm,
    ab_ref, z_ref, s_ref, t_ref, r_ref, h_ref, m_ref, w_ref, k_ref, cs0_ref, cs_ref, ct0_ref, ct_ref, cr0_ref, cr_ref, et0_ref, et_ref, ef0_ref, ef_ref, g_ref, o_ref, e_ref, fz, fy, fx, ix, iy, iz,
    table_sem, in_sem, out_sem, own_sem, zs_sem, zr_sem, fs_sem, fr_sem, bs_sem, br_sem, cs_sem, cr_sem, ts_sem, tr_sem, es_sem, er_sem, fs2_sem, fr2_sem, ek_sem,
):
    me, tm = lax.axis_index("space"), lax.axis_index("tm")
    near = (lax.rem(tm + 7, 8), lax.rem(tm + 1, 8))
    half, cell = me // CELLS, lax.rem(me, CELLS)
    partner = lax.rem(me + CELLS, PEERS)
    far = (1 - half) * CELLS
    at_end = lax.rem(tm, 7) == 0
    other = 7 - tm

    def cell_of(k):
        along_x = lax.rem(cell // 4 + k // 4, 4)
        along_y = lax.rem(lax.rem(cell, 4) + lax.rem(k, 4), 4)
        return 4 * along_x + along_y

    def rows(first, count=1):
        return pl.ds(pl.multiple_of(first * 24, 8), count * 24)

    def remote(src, dst, send, recv, space, time=None):
        return pltpu.make_async_remote_copy(
            src_ref=src,
            dst_ref=dst,
            send_sem=send,
            recv_sem=recv,
            device_id=(tm if time is None else time, space),
            device_id_type=MESH_ID,
        )

    def each_cell(act):
        @pl.loop(1, CELLS)
        def _(k):
            act(cell_of(k))

    def load(f, x):
        return pltpu.make_async_copy((a_hbm, b_hbm)[f].at[x], ab_ref.at[f, x], in_sem.at[f, x])

    tables_hbm = (fz_hbm, fy_hbm, fx_hbm, ix_hbm, iy_hbm, iz_hbm)
    loads = [
        pltpu.make_async_copy(src, dst, table_sem.at[i])
        for i, (src, dst) in enumerate(zip(tables_hbm, (fz, fy, fx, ix, iy, iz)))
    ]
    for f in range(2):
        load(f, 0).start()
    for copy in loads[:2]:
        copy.start()
    for x in range(1, 3):
        for f in range(2):
            load(f, x).start()
    for copy in loads[2:]:
        copy.start()
    barrier = pltpu.get_barrier_semaphore()
    pl.semaphore_signal(barrier, inc=1, device_id=(tm, partner), device_id_type=MESH_ID)
    each_cell(
        lambda to: pl.semaphore_signal(
            barrier, inc=1, device_id=(tm, half * CELLS + to), device_id_type=MESH_ID
        )
    )
    for k in range(2):
        pl.semaphore_signal(barrier, inc=1, device_id=(near[k], me), device_id_type=MESH_ID)

    @pl.when(at_end)
    def _():
        pl.semaphore_signal(barrier, inc=1, device_id=(other, partner), device_id_type=MESH_ID)

    def cross(q, x):
        return remote(s_ref.at[q, x, rows(far, CELLS)], t_ref.at[q, x], zs_sem.at[q, x], zr_sem.at[q, x], partner)

    def spread(q, x, to):
        at = half * CELLS + to
        return remote(s_ref.at[q, x, rows(at)], r_ref.at[q, x, rows(me)], fs_sem.at[0], fr_sem.at[0, q], at)

    def relay(q, x, to):
        at = half * CELLS + to
        return remote(t_ref.at[q, x, rows(to)], r_ref.at[q, x, rows(partner)], fs_sem.at[1], fr_sem.at[1, q], at)

    def keep(q, x):
        return pltpu.make_async_copy(s_ref.at[q, x, rows(me)], r_ref.at[q, x, rows(me)], own_sem.at[0, q, x])

    def keep_relay(q, x):
        return pltpu.make_async_copy(t_ref.at[q, x, rows(cell)], r_ref.at[q, x, rows(partner)], own_sem.at[1, q, x])

    def group(refs, g, first, count=1):
        size = 24 if g else 8
        at = pl.ds(pl.multiple_of(first * size, 8), count * size)
        return refs[1].at[g - 1, at] if g else refs[0].at[at]

    made, passed, final = (cs0_ref, cs_ref), (ct0_ref, ct_ref), (cr0_ref, cr_ref)

    def cross_back(g):
        return remote(group(made, g, far, CELLS), group(passed, g, 0, CELLS), bs_sem.at[g], br_sem.at[g], partner)

    def spread_back(g, to):
        at = half * CELLS + to
        return remote(group(made, g, at), group(final, g, me), cs_sem.at[0, g], cr_sem.at[0, g], at)

    def relay_back(g, to):
        at = half * CELLS + to
        return remote(group(passed, g, to), group(final, g, partner), cs_sem.at[1, g], cr_sem.at[1, g], at)

    def all_back(i, g):
        some = group(final, g, 0, CELLS - 1)
        return remote(some, some, cs_sem.at[i, g], cr_sem.at[i, g], partner)

    def keep_back(g):
        return pltpu.make_async_copy(group(made, g, me), group(final, g, me), own_sem.at[2, g, 0])

    def keep_relay_back(g):
        return pltpu.make_async_copy(group(passed, g, cell), group(final, g, partner), own_sem.at[2, g, 1])

    holders = (me, partner)
    ends = [(et0_ref.at[i], et_ref.at[i]) for i in range(2)]
    end_final = (ef0_ref, ef_ref)

    def cross_end(g, i):
        first = (half * CELLS, far)[i]
        src, dst = group(made, g, first, CELLS), group(ends[i], g, 0, CELLS)
        return remote(src, dst, es_sem.at[i, g], er_sem.at[i, g], holders[i], other)

    def relay_end(g, i, to):
        src, dst = group(ends[i], g, to), group(end_final, g, holders[i])
        return remote(src, dst, fs2_sem.at[i, g], fr2_sem.at[i, g], half * CELLS + to)

    def all_end(i, g):
        some = group(end_final, g, 0, CELLS - 1)
        return remote(some, some, fs2_sem.at[i, g], fr2_sem.at[i, g], partner)

    def keep_end(g, i):
        return pltpu.make_async_copy(group(ends[i], g, cell), group(end_final, g, holders[i]), ek_sem.at[i, g])

    def store_end(x):
        return pltpu.make_async_copy(e_ref.at[x], n_hbm.at[1 - tm // 7, x], ek_sem.at[2, x])

    def send_back(g):
        cross_back(g).start()
        each_cell(lambda to: spread_back(g, to).start())
        keep_back(g).start()

    def time_copy(k, x):
        return remote(o_ref.at[x], n_hbm.at[k, x], ts_sem.at[k, x], tr_sem.at[k, x], me, near[k])

    def store(x):
        return pltpu.make_async_copy(o_ref.at[x], o_hbm.at[x], out_sem.at[x])

    def send(q, x):
        cross(q, x).start()
        each_cell(lambda to: spread(q, x, to).start())
        keep(q, x).start()

    for copy in loads[:2]:
        copy.wait()

    @pl.loop(0, 3)
    def _(x):
        for f in range(2):
            load(f, x).wait()
            depth_step(ab_ref.at[f], x, fz, z_ref, f)

        @pl.loop(0, 8, unroll=4)
        def _(c):
            rows_step(z_ref, fy, x, c, s_ref)

        @pl.when((x == 0) & at_end)
        def _():
            pl.semaphore_wait(barrier, CELLS + 3)

        @pl.when((x == 0) & jnp.logical_not(at_end))
        def _():
            pl.semaphore_wait(barrier, CELLS + 2)

        send(0, x)

    @pl.loop(0, 6)
    def _(i):
        send(1 + i // 3, lax.rem(i, 3))

    every = pl.ds(0, 24 * (CELLS - 1))
    weights_step(pairs_ref, signs_ref, w_ref)
    for copy in loads[2:]:
        copy.wait()

    @pl.loop(0, 3)
    def _(q):
        @pl.loop(0, 3)
        def _(x):
            cross(q, x).wait_recv()
            each_cell(lambda to: relay(q, x, to).start())
            keep_relay(q, x).start()
            keep(q, x).wait()

        for i in range(2):
            remote(r_ref.at[q, :, every], r_ref.at[q, :, every], fs_sem.at[i], fr_sem.at[i, q], partner).wait_recv()

        @pl.loop(0, 3)
        def _(x):
            keep_relay(q, x).wait()

        @pl.loop(0, 8, unroll=4)
        def _(c):
            columns_step(r_ref, q, fx, c, h_ref)

        contract_step(w_ref, h_ref, m_ref)
        columns_back_step(m_ref, ix, q, cs0_ref, cs_ref, k_ref)
        for g in range(3):

            @pl.when(q == g)
            def _():
                send_back(g)

    @pl.when(at_end)
    def _():
        for g, i in ((0, 1), (1, 1), (2, 1)):
            cross_end(g, i).start()

    for g in range(3):
        cross_back(g).wait_recv()
        each_cell(lambda to: relay_back(g, to).start())
        keep_relay_back(g).start()
        keep_back(g).wait()
    for g in range(3):
        for i in range(2):
            all_back(i, g).wait_recv()
        keep_relay_back(g).wait()

    for x in range(3):
        for pair in range(2):
            rows_back_step(cr0_ref, cr_ref, iy, x, pair, g_ref)
        depth_back_step(g_ref, iz, x, o_ref)

        @pl.when(tm > 0)
        def _():
            time_copy(0, x).start()

        @pl.when(tm < 7)
        def _():
            time_copy(1, x).start()

        store(x).start()

    @pl.when(at_end)
    def _():
        for g, i in ((0, 0), (1, 0), (2, 0)):
            cross_end(g, i).start()

    @pl.when(at_end)
    def _():
        for i, g in [(i, g) for i in (1, 0) for g in range(3)]:
            cross_end(g, i).wait_recv()
            each_cell(lambda to: relay_end(g, i, to).start())
            keep_end(g, i).start()
        for g in range(3):
            for i in range(2):
                all_end(i, g).wait_recv()
                keep_end(g, i).wait()
        for x in range(3):
            for pair in range(2):
                rows_back_step(ef0_ref, ef_ref, iy, x, pair, g_ref)
            depth_back_step(g_ref, iz, x, e_ref)
            store_end(x).start()
        for x in range(3):
            store_end(x).wait()
        for g in range(3):
            for i in range(2):
                all_end(i, g).wait_send()
                cross_end(g, i).wait_send()

    for i in range(2):
        remote(s_ref.at[:, :, every], s_ref.at[:, :, every], fs_sem.at[i], fr_sem.at[i, 0], partner).wait_send()
        for g in range(3):
            all_back(i, g).wait_send()
    for g in range(3):
        cross_back(g).wait_send()

    @pl.loop(0, 3)
    def _(q):
        for x in range(3):
            cross(q, x).wait_send()
        store(q).wait()

        @pl.when(tm > 0)
        def _():
            time_copy(0, q).wait_send()
            time_copy(1, q).wait_recv()

        @pl.when(tm < 7)
        def _():
            time_copy(1, q).wait_send()
            time_copy(0, q).wait_recv()


def per_device(field_a, field_b, pairs, signs):
    fy, fx, ix, iy, fz, iz = tables()
    a = jnp.transpose(field_a[0], (1, 0, 2))
    b = jnp.transpose(field_b[0], (1, 0, 2))
    dma = pltpu.SemaphoreType.DMA
    own, others = pl.pallas_call(
        whole_kernel,
        out_shape=[jax.ShapeDtypeStruct((3, 192, 384), F32), jax.ShapeDtypeStruct((2, 3, 192, 384), F32)],
        in_specs=[ANY, ANY, SMEM, SMEM] + [ANY] * 6,
        out_specs=[ANY] * 2,
        scratch_shapes=[
            pltpu.VMEM((2, 3, 8, 18432), F32),
            pltpu.VMEM((2, 3, 4, 384, 128), F32),
            pltpu.VMEM((3, 3, PEERS * 24, 128), F32),
            pltpu.VMEM((3, 3, CELLS * 24, 128), F32),
            pltpu.VMEM((3, 3, PEERS * 24, 128), F32),
            pltpu.VMEM((8, 192, 256), F32),
            pltpu.VMEM((4, 192, 128), F32),
            pltpu.VMEM((256, 8, 128), F32),
            pltpu.VMEM((2, 24, PEERS, 128), F32),
            pltpu.VMEM((PEERS * 8, 128), F32),
            pltpu.VMEM((2, PEERS * 24, 128), F32),
            pltpu.VMEM((CELLS * 8, 128), F32),
            pltpu.VMEM((2, CELLS * 24, 128), F32),
            pltpu.VMEM((PEERS * 8, 128), F32),
            pltpu.VMEM((2, PEERS * 24, 128), F32),
            pltpu.VMEM((2, CELLS * 8, 128), F32),
            pltpu.VMEM((2, 2, CELLS * 24, 128), F32),
            pltpu.VMEM((PEERS * 8, 128), F32),
            pltpu.VMEM((2, PEERS * 24, 128), F32),
            pltpu.VMEM((3, 4, 192, 128), F32),
            pltpu.VMEM((3, 192, 384), F32),
            pltpu.VMEM((3, 192, 384), F32),
            pltpu.VMEM(fz.shape, BF16),
            pltpu.VMEM(fy.shape, BF16),
            pltpu.VMEM(fx.shape, BF16),
            pltpu.VMEM(ix.shape, BF16),
            pltpu.VMEM(iy.shape, BF16),
            pltpu.VMEM(iz.shape, BF16),
            dma((6,)),
            dma((2, 3)),
            dma((3,)),
            dma((3, 3, 3)),
            dma((3, 3)),
            dma((3, 3)),
            dma((2,)),
            dma((2, 3)),
            dma((3,)),
            dma((3,)),
            dma((2, 3)),
            dma((2, 3)),
            dma((2, 3)),
            dma((2, 3)),
            dma((2, 3)),
            dma((2, 3)),
            dma((2, 3)),
            dma((2, 3)),
            dma((3, 3)),
        ],
        compiler_params=pltpu.CompilerParams(vmem_limit_bytes=60_000_000, collective_id=0, has_side_effects=True),
        name="whole",
    )(a, b, jnp.transpose(pairs, (0, 2, 1)), signs, fz, fy, fx, ix, iy, iz)
    outs = pl.pallas_call(
        differences_kernel,
        out_shape=[jax.ShapeDtypeStruct((3, 4, 18432), F32)] * 3,
        in_specs=[ANY] * 2,
        out_specs=[ANY] * 3,
        scratch_shapes=[
            pltpu.VMEM((3, 192, 384), F32),
            pltpu.VMEM((2, 3, 192, 384), F32),
            pltpu.VMEM((3, 3, 4, 18432), F32),
            dma((3, 9)),
            dma((3, 9)),
        ],
        compiler_params=pltpu.CompilerParams(vmem_limit_bytes=62_000_000),
        name="differences",
    )(own, others)
    return tuple(jnp.transpose(out, (1, 0, 2))[None] for out in outs)


def solution(mesh):
    spec = P("tm", None, "space", None)
    return jax.shard_map(
        per_device, mesh=mesh, in_specs=(spec, spec, P(), P()), out_specs=(spec,) * 3, check_vma=False
    )
```
